256 devices in a mesh: view: 8 (over z), gx: 4 (over x), gy: 8 (over y, core).
Axes of the slice: x: 4, y: 4, z: 8, core: 2. Of those that a mesh axis runs over, the one named last changes fastest.
Arguments:
- velocity: float32 [3, 128, 1024, 1024], P(None, 'gx', 'gy', 'view'), may hold values from -6 to 6
- occupied: int32 [16, 128, 8], P('gx', 'gy', 'view'), may hold values 0 or 1
- q_floor: float32 [1], replicated, may hold values from -1 to 0
- q_span: float32 [1], replicated, may hold values from 1 to 4
Outputs:
- image: float32 [4, 8, 4, 32, 128], P('gx', 'gy', None, 'view')
The draws below stay inside these ranges and needn't reach their ends.
All inputs are finite; a program needn't handle non-finite values. No bound on the sum of `occupied` on one device may be relied on, other than what follows from the above.
Results may differ from the reference program's by a relative error of at most 0.0003.
Values sent between devices are 32-bit elements; how exact they have to be, the bound alone decides.
A program may use at most 128 MiB of HBM per device.

```python
import math
import jax
import jax.numpy as jnp
from jax import lax

BX = 32
BY = 128
BZ = 128
SUB = 8
NX = 128
NY = 1024
NZ = 1024
N_VIEW = 8
N_GX = 4
N_GY = 8


def touch_ends(result, key, smallest, high):
    spot = [jax.random.randint(jax.random.fold_in(key, axis), (), 0, length) for axis, length in enumerate(result.shape)]
    longest = result.shape.index(max(result.shape))
    beside = spot[:longest] + [(spot[longest] + 1) % result.shape[longest]] + spot[longest + 1:]
    return result.at[tuple(spot)].set(smallest).at[tuple(beside)].set(high)


def shard_levels(own_key, shape, split, low, top_value):
    def one(dim, parts):
        heights = jax.random.uniform(jax.random.fold_in(jax.random.fold_in(own_key, 6), dim), (parts,), jnp.float32, low / len(split), top_value / len(split))
        return jnp.repeat(jnp.exp(heights), shape[dim] // parts).reshape((-1,) + (1,) * (len(shape) - dim - 1))

    gain = one(*split[0])
    for cut in split[1:]:
        gain = gain * one(*cut)
    return gain


def scatter_about(key, extent, width, limit, cuts=(), kind=jnp.bfloat16):
    loudness = shard_levels(key, extent, cuts, -0.22, 0.18) if cuts else 1.0
    values = jax.random.normal(key, extent, jnp.float32) * width * loudness
    return jnp.minimum(jnp.maximum(values, -limit), limit).astype(kind)


def setup_inputs(seed: int = 0) -> dict:
    streams_of = jax.random.split(jax.random.key(seed), 5)
    velocity = scatter_about(streams_of[0], (3, NX, NY, NZ), 1.0, 6.0, ((1, 4), (2, 8), (3, 8)), jnp.float32)
    occupied = touch_ends((jax.random.randint(streams_of[1], (NX // SUB, NY // SUB, N_VIEW), 0, 4) < 3).astype(jnp.int32), jax.random.fold_in(streams_of[1], 1), 0, 1)
    q_floor = jnp.clip(jax.random.uniform(streams_of[2], (1,), jnp.float32, -1.0, 0.0), -1.0, 0.0)
    q_span = jnp.clip(jnp.exp(jax.random.uniform(streams_of[3], (1,), jnp.float32, math.log(1.0), math.log(4.0))), 1.0, 4.0)
    return dict(velocity=velocity, occupied=occupied, q_floor=q_floor, q_span=q_span)


slab_rows = 8


def derivative(padded_field, direction):
    length_inner = padded_field.shape[direction] - 4

    def shifted(offset):
        return lax.slice_in_dim(padded_field, offset, offset + length_inner, axis=direction)

    return (shifted(0) - 8.0 * shifted(1) + 8.0 * shifted(3) - shifted(4)) / 12.0


def criterion(padded_sets):
    gradient = [[derivative(padded_sets[column][component], column) for column in range(3)] for component in range(3)]
    diagonal_part = gradient[0][0] * gradient[0][0] + gradient[1][1] * gradient[1][1] + gradient[2][2] * gradient[2][2]
    cross_part = gradient[0][1] * gradient[1][0] + gradient[0][2] * gradient[2][0] + gradient[1][2] * gradient[2][1]
    return -0.5 * diagonal_part - cross_part


def reference(velocity, occupied, q_floor, q_span):
    density = 5.0 / NZ
    row_total = velocity.shape[1]

    def one_slab(slab_index):
        first_row = slab_index * slab_rows
        row_index = (first_row - 2 + jnp.arange(slab_rows + 4, dtype=jnp.int32)) % row_total
        slab_cells = jnp.take(velocity, row_index, axis=1)
        middle = slab_cells[:, 2:-2]
        pad_down = jnp.pad(middle, ((0, 0), (0, 0), (2, 2), (0, 0)), mode="wrap")
        pad_depth = jnp.pad(middle, ((0, 0), (0, 0), (0, 0), (2, 2)), mode="wrap")
        qvalue = criterion((slab_cells, pad_down, pad_depth))
        mask_rows = (first_row + jnp.arange(slab_rows, dtype=jnp.int32)) // SUB
        occupancy = jnp.take(occupied, mask_rows, axis=0)
        occupancy = jnp.repeat(jnp.repeat(occupancy, SUB, axis=1), BZ, axis=2).astype(jnp.float32)
        shade_level = jnp.clip((qvalue - q_floor[0]) / q_span[0], 0.0, 1.0) * occupancy
        optical = density * shade_level
        coverage = 1.0 - jnp.exp(-optical)
        passing = jnp.exp(-(jnp.cumsum(optical, axis=-1) - optical))
        weight = passing * coverage
        red = jnp.sum(weight * shade_level, axis=-1)
        green = jnp.sum(weight * 4.0 * shade_level * (1.0 - shade_level), axis=-1)
        blue = jnp.sum(weight * (1.0 - shade_level), axis=-1)
        opacity = 1.0 - jnp.exp(-jnp.sum(optical, axis=-1))
        return jnp.stack([red, green, blue, opacity], axis=0)

    slabs = lax.map(one_slab, jnp.arange(NX // slab_rows, dtype=jnp.int32))
    whole = jnp.moveaxis(slabs, 1, 0).reshape(4, NX, NY)
    return whole.reshape(4, N_GX, BX, N_GY, BY).transpose(1, 3, 0, 2, 4)
```

```python
import functools
import math

import jax
import jax.numpy as jnp
from jax import lax
from jax.experimental import pallas as pl
from jax.experimental.pallas import tpu as pltpu
from jax.sharding import PartitionSpec as P

MESH = pl.DeviceIdType.MESH
SUB = 8
LANES = 128
ROWS = 4
VIEW = 8


def stencil(a, b, c, d):
    return (c - b) - 0.125 * (d - a)


def kernel(
    vel, occ, q_floor, q_span, out,
    cells, packed, send_l, send_r, recv_l, recv_r, edge, split, lower, trans, gain, parts, arrived,
    load_sem, halo_send, halo_recv, z_send, z_recv, part_send, part_recv,
):
    v = lax.axis_index("view")
    gx = lax.axis_index("gx")
    gy = lax.axis_index("gy")
    n_gx, n_gy = lax.axis_size("gx"), lax.axis_size("gy")
    v_next, v_prev = lax.rem(v + 1, VIEW), lax.rem(v + VIEW - 1, VIEW)
    x_next, x_prev = lax.rem(gx + 1, n_gx), lax.rem(gx + n_gx - 1, n_gx)
    y_next, y_prev = lax.rem(gy + 1, n_gy), lax.rem(gy + n_gy - 1, n_gy)

    loads = []
    for g in range(2):
        for c in range(3):
            load = pltpu.make_async_copy(
                vel.at[c, pl.ds(16 * g, 16)],
                cells.at[c, pl.ds(2 + 16 * g, 16), pl.ds(8, 128)],
                load_sem.at[g, c],
            )
            load.start()
            loads.append(load)

    barrier = pltpu.get_barrier_semaphore()
    for target in ({"gx": x_next}, {"gx": x_prev}, {"gy": y_next}, {"gy": y_prev}):
        pl.semaphore_signal(barrier, inc=1, device_id=target, device_id_type=MESH)
    for step in range(1, VIEW):
        pl.semaphore_signal(
            barrier, inc=1, device_id={"view": lax.rem(v + step, VIEW)}, device_id_type=MESH
        )
    pl.semaphore_wait(barrier, 4 + VIEW - 1)

    halos = []

    def send_halo(number, src, dst, target):
        copy = pltpu.make_async_remote_copy(
            src_ref=src, dst_ref=dst, send_sem=halo_send.at[number], recv_sem=halo_recv.at[number],
            device_id=target, device_id_type=MESH,
        )
        copy.start()
        halos.append(copy)

    body = pl.ds(8, 128)
    send_halo(0, vel.at[:, pl.ds(0, 2)], cells.at[:, pl.ds(34, 2), body], {"gx": x_prev})
    send_halo(1, vel.at[:, pl.ds(30, 2)], cells.at[:, pl.ds(0, 2), body], {"gx": x_next})
    send_halo(2, vel.at[:, :, pl.ds(0, 2)], cells.at[:, pl.ds(2, 32), pl.ds(136, 2)], {"gy": y_prev})
    send_halo(3, vel.at[:, :, pl.ds(126, 2)], cells.at[:, pl.ds(2, 32), pl.ds(6, 2)], {"gy": y_next})

    lane = lax.broadcasted_iota(jnp.int32, (8, LANES), 1)
    slot = lane % 8
    block = lane // 8
    row_id = lax.broadcasted_iota(jnp.int32, (256, 256), 0)
    col_id = lax.broadcasted_iota(jnp.int32, (256, 256), 1)
    depth_of = col_id % LANES
    chosen = ((row_id < LANES) & (depth_of < row_id)) | (depth_of == row_id - LANES)
    lower[...] = chosen.astype(jnp.float32).astype(jnp.bfloat16)

    def pack(g):
        bits = [(block // (1 << n)) % 2 == 1 for n in range(4)]

        @pl.loop(0, 16)
        def _(t):
            rows = pl.ds(pl.multiple_of(8 + 8 * t, 8), 8)
            own = pl.ds(pl.multiple_of(8 * t, 8), 8)
            left = jnp.zeros((8, LANES), jnp.float32)
            right = jnp.zeros((8, LANES), jnp.float32)
            for c in range(3):
                terms = [
                    pltpu.roll(cells[c, 2 + 16 * g + x, rows], (8 * x + 4) % LANES, 1)
                    for x in range(16)
                ]
                for n in range(4):
                    terms = [
                        jnp.where(bits[n], terms[2 * i + 1], terms[2 * i])
                        for i in range(len(terms) // 2)
                    ]
                packed[g, c, own] = terms[0]
                here = slot // 2 == c
                left = jnp.where(here, pltpu.roll(terms[0], (2 * c - 4) % LANES, 1), left)
                right = jnp.where(here, pltpu.roll(terms[0], (2 * c - 2) % LANES, 1), right)
            send_l[g, own] = left
            send_r[g, own] = right

    z_copies = []
    for g in range(2):
        for c in range(3):
            loads[3 * g + c].wait()
        pack(g)
        for side, (src, dst, target) in enumerate(
            ((send_l, recv_l, {"view": v_prev}), (send_r, recv_r, {"view": v_next}))
        ):
            copy = pltpu.make_async_remote_copy(
                src_ref=src.at[g], dst_ref=dst.at[g], send_sem=z_send.at[g, side],
                recv_sem=z_recv.at[g, side], device_id=target, device_id_type=MESH,
            )
            copy.start()
            z_copies.append(copy)

    for g in range(2):
        for copy in z_copies[2 * g : 2 * g + 2]:
            copy.wait_recv()

        @pl.loop(0, 16)
        def _(t):
            own = pl.ds(pl.multiple_of(8 * t, 8), 8)
            after, before = recv_l[g, own], recv_r[g, own]
            for c in range(3):
                mine = packed[g, c, own]
                upper = jnp.where(slot // 2 == 2, pltpu.roll(after, (4 - 2 * c) % LANES, 1), mine)
                under = jnp.where(slot // 2 == 1, pltpu.roll(before, (2 - 2 * c) % LANES, 1), mine)

                def along(w):
                    return stencil(
                        pltpu.roll(w, 2, 1), pltpu.roll(w, 1, 1),
                        pltpu.roll(w, LANES - 1, 1), pltpu.roll(w, LANES - 2, 1),
                    )

                edge[g, c, own] = jnp.where(slot < 4, along(upper), along(under))

    for copy in halos:
        copy.wait_recv()

    unit = -(5.0 / (LANES * VIEW)) * math.log2(math.e)
    slope = -unit / (4.5 * q_span[0])
    shift = -unit * q_floor[0] / q_span[0]

    rim = (lane < 2) | (lane >= LANES - 2)
    rim16 = jnp.concatenate([rim, rim], axis=0)

    def level_of(b, k, t):
        x = 4 * b + k + 2
        top = 8 + 16 * t
        g = b // 4
        turn = 124 - 32 * (b % 4) - 8 * k
        grad = []
        for c in range(3):
            def at(dx, dy):
                return cells[c, x + dx, pl.ds(top + dy, 16)]

            mine = at(0, 0)
            across = stencil(at(-2, 0), at(-1, 0), at(1, 0), at(2, 0))
            down = stencil(at(0, -2), at(0, -1), at(0, 1), at(0, 2))
            ahead = pltpu.roll(mine, LANES - 2, 1) - mine
            deep = pltpu.roll(ahead, 1, 1) - 0.125 * (ahead + pltpu.roll(ahead, 2, 1))
            ends = pltpu.roll(edge[g, c, pl.ds(16 * t, 16)], turn, 1)
            deep = jnp.where(rim16, ends, deep)
            grad.append((across, down, deep))
        squares = grad[0][0] * grad[0][0] + grad[1][1] * grad[1][1] + grad[2][2] * grad[2][2]
        cross = grad[0][1] * grad[1][0] + grad[0][2] * grad[2][0] + grad[1][2] * grad[2][1]
        total = (squares + cross) + cross
        factors = []
        for half in range(2):
            keep = occ[b // 2, 0, 2 * t + half].astype(jnp.float32)
            factors.append((slope * keep, shift * keep))
        m = jnp.concatenate([jnp.full((8, LANES), f[0], jnp.float32) for f in factors], axis=0)
        s = jnp.concatenate([jnp.full((8, LANES), f[1], jnp.float32) for f in factors], axis=0)
        return jnp.maximum(jnp.minimum(total * m + s, 0.0), unit)

    def block_of(step):
        far = 4 + jnp.where(step % 2 == 1, -1, 1) * ((step + 1) // 2)
        return (v + far) % VIEW

    def do_block(step):
        b = block_of(step)
        for k in range(ROWS):
            for t in range(8):
                lev = level_of(b, k, t)
                high = lev.astype(jnp.bfloat16)
                low = (lev - high.astype(jnp.float32)).astype(jnp.bfloat16)
                here = pl.ds(128 * (k % 2) + 16 * t, 16)
                split[k // 2, here, pl.ds(0, LANES)] = high
                split[k // 2, here, pl.ds(LANES, LANES)] = low
        for pair in range(2):
            turned = lax.dot_general(
                lower[...], split[pair], (((1,), (1,)), ((), ())),
                preferred_element_type=jnp.float32,
            )
            first = jnp.zeros((8, 256), jnp.float32)
            second = jnp.zeros((8, 256), jnp.float32)
            for z in range(16):
                passing = jnp.exp2(turned[8 * z : 8 * z + 8])
                lev = turned[128 + 8 * z : 136 + 8 * z]
                left = passing * jnp.exp2(lev)
                one = (passing - left) * lev
                first = first + one
                second = second + one * lev
            rows = [
                jnp.sum(first, axis=0, keepdims=True),
                jnp.sum(second, axis=0, keepdims=True),
                left[7:8],
            ]
            for q in range(3):
                for k in range(2):
                    parts[step, pl.ds(4 * q + 2 * pair + k, 1)] = rows[q][:, 128 * k : 128 * k + 128]
        return b

    def part_copy(step):
        far = 4 + jnp.where(step % 2 == 1, -1, 1) * ((step + 1) // 2)
        return pltpu.make_async_remote_copy(
            src_ref=parts.at[step], dst_ref=arrived.at[v], send_sem=part_send.at[step],
            recv_sem=part_recv.at[step], device_id={"view": (v + far) % VIEW},
            device_id_type=MESH,
        )

    @pl.loop(0, VIEW - 1)
    def _(step):
        do_block(step)
        part_copy(step).start()

    do_block(VIEW - 1)
    arrived[v] = parts[VIEW - 1]

    for step in range(VIEW - 1):
        part_copy(step).wait_recv()

    red = jnp.zeros((ROWS, LANES), jnp.float32)
    green = jnp.zeros((ROWS, LANES), jnp.float32)
    ahead = jnp.ones((ROWS, LANES), jnp.float32)
    for s in range(VIEW):
        red = red + ahead * arrived[s, 0:4]
        green = green + ahead * arrived[s, 4:8]
        ahead = ahead * arrived[s, 8:12]
    red = red * (1.0 / unit)
    green = 4.0 * (red - green * (1.0 / (unit * unit)))
    out[0, 0, 0] = red
    out[0, 0, 1] = green
    out[0, 0, 2] = (1.0 - ahead) - red
    out[0, 0, 3] = 1.0 - ahead

    for copy in halos + z_copies:
        copy.wait_send()
    for step in range(VIEW - 1):
        part_copy(step).wait_send()


def local(velocity, occupied, q_floor, q_span):
    f32, bf16 = jnp.float32, jnp.bfloat16
    smem = pl.BlockSpec(memory_space=pltpu.SMEM)
    return pl.pallas_call(
        kernel,
        out_shape=jax.ShapeDtypeStruct((1, 1, 4, ROWS, LANES), f32),
        in_specs=[pl.BlockSpec(memory_space=pl.ANY), smem, smem, smem],
        out_specs=pl.BlockSpec(memory_space=pltpu.VMEM),
        scratch_shapes=[
            pltpu.VMEM((3, 36, 144, LANES), f32),
            pltpu.VMEM((2, 3, 128, LANES), f32),
            pltpu.VMEM((2, 128, LANES), f32),
            pltpu.VMEM((2, 128, LANES), f32),
            pltpu.VMEM((2, 128, LANES), f32),
            pltpu.VMEM((2, 128, LANES), f32),
            pltpu.VMEM((2, 3, 128, LANES), f32),
            pltpu.VMEM((2, 256, 256), bf16),
            pltpu.VMEM((256, 256), bf16),
            pltpu.VMEM((8, LANES), f32),
            pltpu.VMEM((8, LANES), f32),
            pltpu.VMEM((VIEW, 16, LANES), f32),
            pltpu.VMEM((VIEW, 16, LANES), f32),
            pltpu.SemaphoreType.DMA((2, 3)),
            pltpu.SemaphoreType.DMA((4,)),
            pltpu.SemaphoreType.DMA((4,)),
            pltpu.SemaphoreType.DMA((2, 2)),
            pltpu.SemaphoreType.DMA((2, 2)),
            pltpu.SemaphoreType.DMA((VIEW - 1,)),
            pltpu.SemaphoreType.DMA((VIEW - 1,)),
        ],
        compiler_params=pltpu.CompilerParams(collective_id=0, has_side_effects=True),
    )(velocity, occupied.transpose(0, 2, 1), q_floor, q_span)


def solution(mesh):
    placed = (P(None, "gx", "gy", "view"), P("gx", "gy", "view"), P(), P())
    return jax.shard_map(
        local,
        mesh=mesh,
        in_specs=placed,
        out_specs=P("gx", "gy", None, "view", None),
        check_vma=False,
    )
```

```python
import functools
import math

import jax
import jax.numpy as jnp
from jax import lax
from jax.experimental import pallas as pl
from jax.experimental.pallas import tpu as pltpu
from jax.sharding import PartitionSpec as P

MESH = pl.DeviceIdType.MESH
SUB = 8
LANES = 128
ROWS = 4
VIEW = 8


def stencil(a, b, c, d):
    return (c - b) - 0.125 * (d - a)


def kernel(
    vel, occ, q_floor, q_span, out,
    cells, pieces, stencils, send_l, send_r, recv_l, recv_r, deep_ref, split, lower, parts, arrived,
    load_sem, halo_send, halo_recv, z_send, z_recv, part_send, part_recv, ready,
):
    f32, bf16 = jnp.float32, jnp.bfloat16
    v = lax.axis_index("view")
    gx = lax.axis_index("gx")
    gy = lax.axis_index("gy")
    n_gx, n_gy = lax.axis_size("gx"), lax.axis_size("gy")

    def view(step):
        return lax.rem(v + VIEW + step, VIEW)

    x_next, x_prev = lax.rem(gx + 1, n_gx), lax.rem(gx + n_gx - 1, n_gx)
    y_next, y_prev = lax.rem(gy + 1, n_gy), lax.rem(gy + n_gy - 1, n_gy)

    loads = []
    for g in range(2):
        for c in range(3):
            load = pltpu.make_async_copy(
                vel.at[c, pl.ds(16 * g, 16)],
                cells.at[c, pl.ds(2 + 16 * g, 16), pl.ds(8, 128)],
                load_sem.at[g, c],
            )
            load.start()
            loads.append(load)

    barrier = pltpu.get_barrier_semaphore()
    for target in (
        {"gx": x_next}, {"gx": x_prev}, {"gy": y_next}, {"gy": y_prev},
        {"view": view(1)}, {"view": view(-1)},
    ):
        pl.semaphore_signal(barrier, inc=1, device_id=target, device_id_type=MESH)
    pl.semaphore_wait(barrier, 6)

    halos = []

    def send_halo(number, src, dst, target):
        copy = pltpu.make_async_remote_copy(
            src_ref=src, dst_ref=dst, send_sem=halo_send.at[number], recv_sem=halo_recv.at[number],
            device_id=target, device_id_type=MESH,
        )
        copy.start()
        halos.append(copy)

    body = pl.ds(8, 128)
    send_halo(0, vel.at[:, pl.ds(0, 2)], cells.at[:, pl.ds(34, 2), body], {"gx": x_prev})
    send_halo(1, vel.at[:, pl.ds(30, 2)], cells.at[:, pl.ds(0, 2), body], {"gx": x_next})
    send_halo(2, vel.at[:, :, pl.ds(0, 2)], cells.at[:, pl.ds(2, 32), pl.ds(136, 2)], {"gy": y_prev})
    send_halo(3, vel.at[:, :, pl.ds(126, 2)], cells.at[:, pl.ds(2, 32), pl.ds(6, 2)], {"gy": y_next})

    row_id = lax.broadcasted_iota(jnp.int32, (256, 256), 0)
    col_id = lax.broadcasted_iota(jnp.int32, (256, 256), 1)
    depth_of = col_id % LANES
    chosen = ((row_id < LANES) & (depth_of < row_id)) | (depth_of == row_id - LANES)
    lower[...] = chosen.astype(f32).astype(bf16)

    to = lax.broadcasted_iota(jnp.int32, (LANES, LANES), 1)
    row = lax.broadcasted_iota(jnp.int32, (LANES, LANES), 0)

    def weight(gap):
        near = (gap == 1).astype(f32) - (gap == -1).astype(f32)
        far = (gap == 2).astype(f32) - (gap == -2).astype(f32)
        return (near - 0.125 * far).astype(bf16)

    own_weight = weight(row - to)
    halo_at = jnp.where(row % 4 < 2, row % 4 - 2, row % 4 + LANES - 2)
    halo_weight = weight(halo_at - to)
    for c in range(3):
        for n in range(3):
            stencils[c, pl.ds(LANES * n, LANES)] = own_weight
        stencils[c, pl.ds(3 * LANES, LANES)] = jnp.where(
            row // 8 == c, halo_weight, jnp.zeros_like(halo_weight)
        )

    lane = lax.broadcasted_iota(jnp.int32, (16, LANES), 1)
    pair_of = (lane % 8) // 2

    def pack(g):
        @pl.loop(0, 8)
        def _(t):
            rows = pl.ds(pl.multiple_of(8 + 16 * t, 8), 16)
            own = pl.ds(pl.multiple_of(16 * t, 16), 16)
            gathered = [jnp.zeros((16, LANES), f32) for s in range(4)]
            for k in range(4):
                for c in range(3):
                    here = lane // 8 == 4 * k + c
                    for s in range(4):
                        x = 16 * g + 4 * s + k
                        u = cells[c, 2 + x, rows]
                        high = u.astype(bf16)
                        rest = u - high.astype(f32)
                        mid = rest.astype(bf16)
                        low = (rest - mid.astype(f32)).astype(bf16)
                        pieces[c, x, own, pl.ds(0, LANES)] = high
                        pieces[c, x, own, pl.ds(LANES, LANES)] = mid
                        pieces[c, x, own, pl.ds(2 * LANES, LANES)] = low
                        moved = pltpu.roll(u, (32 * k + 8 * c + 4) % LANES, 1)
                        gathered[s] = jnp.where(here, moved, gathered[s])
            left = right = None
            for s in range(4):
                turned = gathered[s] if s == 2 else pltpu.roll(gathered[s], (2 * s - 4) % LANES, 1)
                left = turned if s == 0 else jnp.where(pair_of == s, turned, left)
                right = turned if s == 0 else jnp.where(pair_of == (s + 3) % 4, turned, right)
            send_l[g, own] = left
            send_r[g, own] = right

    z_copies = []
    for g in range(2):
        for c in range(3):
            loads[3 * g + c].wait()
        pack(g)
        for side, (src, dst, step) in enumerate(((send_l, recv_l, -1), (send_r, recv_r, 1))):
            copy = pltpu.make_async_remote_copy(
                src_ref=src.at[g], dst_ref=dst.at[g], send_sem=z_send.at[g, side],
                recv_sem=z_recv.at[g, side], device_id={"view": view(step)}, device_id_type=MESH,
            )
            copy.start()
            z_copies.append(copy)

    for g in range(2):
        for copy in z_copies[2 * g : 2 * g + 2]:
            copy.wait_recv()

        @pl.loop(0, 8)
        def _(t):
            own = pl.ds(pl.multiple_of(16 * t, 16), 16)
            after, before = recv_l[g, own], recv_r[g, own]
            for s in range(4):
                both = jnp.where(pair_of == s, after, before)
                high = both.astype(bf16).astype(f32)
                rest = pltpu.roll(both - high, 4, 1)
                used = (pair_of == s) | (pair_of == (s + 3) % 4)
                halo = jnp.where(used, high, rest)
                for k in range(4):
                    placed = pltpu.roll(halo, (2 - 32 * k - 2 * s) % LANES, 1).astype(bf16)
                    for c in range(3):
                        pieces[c, 16 * g + 4 * s + k, own, pl.ds(3 * LANES, LANES)] = placed

    for step in (2, -2):
        pl.semaphore_signal(ready, inc=1, device_id={"view": view(step)}, device_id_type=MESH)

    for copy in halos[2:]:
        copy.wait_recv()

    unit = -(5.0 / (LANES * VIEW)) * math.log2(math.e)
    slope = -unit / (4.5 * q_span[0])
    shift = -unit * q_floor[0] / q_span[0]

    def level_of(p, k, t):
        x = 2 * p + k + 2
        top = 8 + 16 * t
        grad = []
        for c in range(3):
            def at(dx, dy):
                return cells[c, x + dx, pl.ds(top + dy, 16)]

            across = stencil(at(-2, 0), at(-1, 0), at(1, 0), at(2, 0))
            down = stencil(at(0, -2), at(0, -1), at(0, 1), at(0, 2))
            deep = deep_ref[c, pl.ds(128 * k + 16 * t, 16)]
            grad.append((across, down, deep))
        squares = grad[0][0] * grad[0][0] + grad[1][1] * grad[1][1] + grad[2][2] * grad[2][2]
        cross = grad[0][1] * grad[1][0] + grad[0][2] * grad[2][0] + grad[1][2] * grad[2][1]
        total = (squares + cross) + cross
        factors = []
        for half in range(2):
            keep = occ[p // 4, 0, 2 * t + half].astype(f32)
            factors.append((slope * keep, shift * keep))
        m = jnp.concatenate([jnp.full((8, LANES), f[0], f32) for f in factors], axis=0)
        s = jnp.concatenate([jnp.full((8, LANES), f[1], f32) for f in factors], axis=0)
        return jnp.maximum(jnp.minimum(total * m + s, 0.0), unit)

    def do_pair(p, odd):
        for c in range(3):
            deep_ref[c] = jnp.dot(
                pieces[c, pl.ds(2 * p, 2)].reshape(256, 4 * LANES), stencils[c],
                preferred_element_type=f32,
            )
        for k in range(2):
            for t in range(8):
                lev = level_of(p, k, t)
                high = lev.astype(bf16)
                low = (lev - high.astype(f32)).astype(bf16)
                here = pl.ds(128 * k + 16 * t, 16)
                split[here, pl.ds(0, LANES)] = high
                split[here, pl.ds(LANES, LANES)] = low
        turned = lax.dot_general(
            lower[...], split[...], (((1,), (1,)), ((), ())), preferred_element_type=f32
        )
        first = jnp.zeros((8, 256), f32)
        second = jnp.zeros((8, 256), f32)
        for z in range(16):
            passing = jnp.exp2(turned[8 * z : 8 * z + 8])
            lev = turned[128 + 8 * z : 136 + 8 * z]
            left = passing * jnp.exp2(lev)
            one = (passing - left) * lev
            first = first + one
            second = second + one * lev
        rows = [
            jnp.sum(first, axis=0, keepdims=True),
            jnp.sum(second, axis=0, keepdims=True),
            left[7:8],
        ]
        for q in range(3):
            for k in range(2):
                parts[p // 2, pl.ds(4 * q + 2 * odd + k, 1)] = rows[q][:, 128 * k : 128 * k + 128]

    def part_copy(b, source):
        return pltpu.make_async_remote_copy(
            src_ref=parts.at[b], dst_ref=arrived.at[source], send_sem=part_send.at[b],
            recv_sem=part_recv.at[source], device_id={"view": b}, device_id_type=MESH,
        )

    def hand_over(b):
        @pl.when(b != v)
        def _():
            part_copy(b, v).start()

        @pl.when(b == v)
        def _():
            arrived[v] = parts[b]

    pl.semaphore_wait(ready, 2)

    @pl.loop(1, VIEW - 1)
    def _(b):
        do_pair(2 * b, 0)
        do_pair(2 * b + 1, 1)
        hand_over(b)

    @pl.loop(0, 2)
    def _(i):
        do_pair(1 + 13 * i, 1 - i)

    for copy in halos[:2]:
        copy.wait_recv()

    @pl.loop(0, 2)
    def _(i):
        last = (i + jnp.where(v < 4, 1, 0)) % 2
        do_pair(15 * last, last)
        hand_over(7 * last)

    for step in range(1, VIEW):
        part_copy(view(step), view(step)).wait_recv()

    red = jnp.zeros((ROWS, LANES), f32)
    green = jnp.zeros((ROWS, LANES), f32)
    ahead = jnp.ones((ROWS, LANES), f32)
    for s in range(VIEW):
        red = red + ahead * arrived[s, 0:4]
        green = green + ahead * arrived[s, 4:8]
        ahead = ahead * arrived[s, 8:12]
    red = red * (1.0 / unit)
    green = 4.0 * (red - green * (1.0 / (unit * unit)))
    out[0, 0, 0] = red
    out[0, 0, 1] = green
    out[0, 0, 2] = (1.0 - ahead) - red
    out[0, 0, 3] = 1.0 - ahead

    for copy in halos + z_copies:
        copy.wait_send()
    for step in range(1, VIEW):
        part_copy(view(step), v).wait_send()


def local(velocity, occupied, q_floor, q_span):
    f32, bf16 = jnp.float32, jnp.bfloat16
    smem = pl.BlockSpec(memory_space=pltpu.SMEM)
    return pl.pallas_call(
        kernel,
        out_shape=jax.ShapeDtypeStruct((1, 1, 4, ROWS, LANES), f32),
        in_specs=[pl.BlockSpec(memory_space=pl.ANY), smem, smem, smem],
        out_specs=pl.BlockSpec(memory_space=pltpu.VMEM),
        scratch_shapes=[
            pltpu.VMEM((3, 36, 144, LANES), f32),
            pltpu.VMEM((3, 32, 128, 4 * LANES), bf16),
            pltpu.VMEM((3, 4 * LANES, LANES), bf16),
            pltpu.VMEM((2, 128, LANES), f32),
            pltpu.VMEM((2, 128, LANES), f32),
            pltpu.VMEM((2, 128, LANES), f32),
            pltpu.VMEM((2, 128, LANES), f32),
            pltpu.VMEM((3, 256, LANES), f32),
            pltpu.VMEM((256, 256), bf16),
            pltpu.VMEM((256, 256), bf16),
            pltpu.VMEM((VIEW, 16, LANES), f32),
            pltpu.VMEM((VIEW, 16, LANES), f32),
            pltpu.SemaphoreType.DMA((2, 3)),
            pltpu.SemaphoreType.DMA((4,)),
            pltpu.SemaphoreType.DMA((4,)),
            pltpu.SemaphoreType.DMA((2, 2)),
            pltpu.SemaphoreType.DMA((2, 2)),
            pltpu.SemaphoreType.DMA((VIEW,)),
            pltpu.SemaphoreType.DMA((VIEW,)),
            pltpu.SemaphoreType.REGULAR,
        ],
        compiler_params=pltpu.CompilerParams(collective_id=0, has_side_effects=True),
    )(velocity, occupied.transpose(0, 2, 1), q_floor, q_span)


def solution(mesh):
    placed = (P(None, "gx", "gy", "view"), P("gx", "gy", "view"), P(), P())
    return jax.shard_map(
        local,
        mesh=mesh,
        in_specs=placed,
        out_specs=P("gx", "gy", None, "view", None),
        check_vma=False,
    )
```

```python
import functools
import math

import jax
import jax.numpy as jnp
from jax import lax
from jax.experimental import pallas as pl
from jax.experimental.pallas import tpu as pltpu
from jax.sharding import PartitionSpec as P

MESH = pl.DeviceIdType.MESH
SUB = 8
LANES = 128
ROWS = 4
VIEW = 8


def stencil(a, b, c, d):
    return (c - b) - 0.125 * (d - a)


def kernel(
    vel, occ_in, q_floor_in, q_span_in, out,
    cells, pieces, stencils, send_l, send_r, recv_l, recv_r, deep_ref, split, lower, parts, arrived,
    load_sem, halo_send, halo_recv, z_send, z_recv, part_send, part_recv, ready,
    occ, q_floor, q_span, small_sem,
):
    f32, bf16 = jnp.float32, jnp.bfloat16
    v = lax.axis_index("view")
    gx = lax.axis_index("gx")
    gy = lax.axis_index("gy")
    n_gx, n_gy = lax.axis_size("gx"), lax.axis_size("gy")

    def view(step):
        return lax.rem(v + VIEW + step, VIEW)

    x_next, x_prev = lax.rem(gx + 1, n_gx), lax.rem(gx + n_gx - 1, n_gx)
    y_next, y_prev = lax.rem(gy + 1, n_gy), lax.rem(gy + n_gy - 1, n_gy)

    loads = []
    for g in range(2):
        for c in range(3):
            load = pltpu.make_async_copy(
                vel.at[c, pl.ds(16 * g, 16)],
                cells.at[c, pl.ds(2 + 16 * g, 16), pl.ds(8, 128)],
                load_sem.at[g, c],
            )
            load.start()
            loads.append(load)

    small = []
    for n, (src, dst) in enumerate(((occ_in, occ), (q_floor_in, q_floor), (q_span_in, q_span))):
        copy = pltpu.make_async_copy(src, dst, small_sem.at[n])
        copy.start()
        small.append(copy)

    barrier = pltpu.get_barrier_semaphore()
    for target in (
        {"gx": x_next}, {"gx": x_prev}, {"gy": y_next}, {"gy": y_prev},
        {"view": view(1)}, {"view": view(-1)},
    ):
        pl.semaphore_signal(barrier, inc=1, device_id=target, device_id_type=MESH)

    row_id = lax.broadcasted_iota(jnp.int32, (256, 256), 0)
    col_id = lax.broadcasted_iota(jnp.int32, (256, 256), 1)
    depth_of = col_id % LANES
    chosen = ((row_id < LANES) & (depth_of < row_id)) | (depth_of == row_id - LANES)
    lower[...] = chosen.astype(f32).astype(bf16)

    to = lax.broadcasted_iota(jnp.int32, (LANES, LANES), 1)
    row = lax.broadcasted_iota(jnp.int32, (LANES, LANES), 0)

    def weight(gap):
        near = (gap == 1).astype(f32) - (gap == -1).astype(f32)
        far = (gap == 2).astype(f32) - (gap == -2).astype(f32)
        return (near - 0.125 * far).astype(bf16)

    own_weight = weight(row - to)
    halo_at = jnp.where(row % 4 < 2, row % 4 - 2, row % 4 + LANES - 2)
    halo_weight = weight(halo_at - to)
    for c in range(3):
        for n in range(3):
            stencils[c, pl.ds(LANES * n, LANES)] = own_weight
        stencils[c, pl.ds(3 * LANES, LANES)] = jnp.where(
            row // 8 == c, halo_weight, jnp.zeros_like(halo_weight)
        )

    lane = lax.broadcasted_iota(jnp.int32, (16, LANES), 1)
    pair_of = (lane % 8) // 2

    def pack(g):
        @pl.loop(0, 8)
        def _(t):
            rows = pl.ds(pl.multiple_of(8 + 16 * t, 8), 16)
            own = pl.ds(pl.multiple_of(16 * t, 16), 16)
            gathered = [jnp.zeros((16, LANES), f32) for s in range(4)]
            for k in range(4):
                for c in range(3):
                    here = lane // 8 == 4 * k + c
                    for s in range(4):
                        x = 16 * g + 4 * s + k
                        u = cells[c, 2 + x, rows]
                        high = u.astype(bf16)
                        rest = u - high.astype(f32)
                        mid = rest.astype(bf16)
                        low = (rest - mid.astype(f32)).astype(bf16)
                        pieces[c, x, own, pl.ds(0, LANES)] = high
                        pieces[c, x, own, pl.ds(LANES, LANES)] = mid
                        pieces[c, x, own, pl.ds(2 * LANES, LANES)] = low
                        moved = pltpu.roll(u, (32 * k + 8 * c + 4) % LANES, 1)
                        gathered[s] = jnp.where(here, moved, gathered[s])
            left = right = None
            for s in range(4):
                turned = gathered[s] if s == 2 else pltpu.roll(gathered[s], (2 * s - 4) % LANES, 1)
                left = turned if s == 0 else jnp.where(pair_of == s, turned, left)
                right = turned if s == 0 else jnp.where(pair_of == (s + 3) % 4, turned, right)
            send_l[g, own] = left
            send_r[g, own] = right

    halos = []

    def enter():
        pl.semaphore_wait(barrier, 6)


        def send_halo(number, src, dst, target):
            copy = pltpu.make_async_remote_copy(
                src_ref=src, dst_ref=dst, send_sem=halo_send.at[number], recv_sem=halo_recv.at[number],
                device_id=target, device_id_type=MESH,
            )
            copy.start()
            halos.append(copy)

        body = pl.ds(8, 128)
        send_halo(0, vel.at[:, pl.ds(0, 2)], cells.at[:, pl.ds(34, 2), body], {"gx": x_prev})
        send_halo(1, vel.at[:, pl.ds(30, 2)], cells.at[:, pl.ds(0, 2), body], {"gx": x_next})
        send_halo(2, vel.at[:, :, pl.ds(0, 2)], cells.at[:, pl.ds(2, 32), pl.ds(136, 2)], {"gy": y_prev})
        send_halo(3, vel.at[:, :, pl.ds(126, 2)], cells.at[:, pl.ds(2, 32), pl.ds(6, 2)], {"gy": y_next})

    z_copies = []
    for g in range(2):
        for c in range(3):
            loads[3 * g + c].wait()
        pack(g)
        if g == 0:
            enter()
        for side, (src, dst, step) in enumerate(((send_l, recv_l, -1), (send_r, recv_r, 1))):
            copy = pltpu.make_async_remote_copy(
                src_ref=src.at[g], dst_ref=dst.at[g], send_sem=z_send.at[g, side],
                recv_sem=z_recv.at[g, side], device_id={"view": view(step)}, device_id_type=MESH,
            )
            copy.start()
            z_copies.append(copy)

    for g in range(2):
        for copy in z_copies[2 * g : 2 * g + 2]:
            copy.wait_recv()

        @pl.loop(0, 8)
        def _(t):
            own = pl.ds(pl.multiple_of(16 * t, 16), 16)
            after, before = recv_l[g, own], recv_r[g, own]
            for s in range(4):
                both = jnp.where(pair_of == s, after, before)
                high = both.astype(bf16).astype(f32)
                rest = pltpu.roll(both - high, 4, 1)
                used = (pair_of == s) | (pair_of == (s + 3) % 4)
                halo = jnp.where(used, high, rest)
                for k in range(4):
                    placed = pltpu.roll(halo, (2 - 32 * k - 2 * s) % LANES, 1).astype(bf16)
                    for c in range(3):
                        pieces[c, 16 * g + 4 * s + k, own, pl.ds(3 * LANES, LANES)] = placed

    for step in (2, -2):
        pl.semaphore_signal(ready, inc=1, device_id={"view": view(step)}, device_id_type=MESH)

    for copy in halos[2:]:
        copy.wait_recv()

    for copy in small:
        copy.wait()

    unit = -(5.0 / (LANES * VIEW)) * math.log2(math.e)
    slope = -unit / (4.5 * q_span[0, 0])
    shift = -unit * q_floor[0, 0] / q_span[0, 0]

    def level_of(p, odd, k, t):
        x = 2 * p + k + 2
        top = 8 + 16 * t
        grad = []
        for c in range(3):
            def at(dx, dy):
                return cells[c, x + dx, pl.ds(top + dy, 16)]

            across = stencil(at(-2, 0), at(-1, 0), at(1, 0), at(2, 0))
            down = stencil(at(0, -2), at(0, -1), at(0, 1), at(0, 2))
            deep = deep_ref[odd, c, pl.ds(128 * k + 16 * t, 16)]
            grad.append((across, down, deep))
        squares = grad[0][0] * grad[0][0] + grad[1][1] * grad[1][1] + grad[2][2] * grad[2][2]
        cross = grad[0][1] * grad[1][0] + grad[0][2] * grad[2][0] + grad[1][2] * grad[2][1]
        total = (squares + cross) + cross
        factors = []
        for half in range(2):
            keep = occ[p // 4, 0, 2 * t + half].astype(f32)
            factors.append((slope * keep, shift * keep))
        m = jnp.concatenate([jnp.full((8, LANES), f[0], f32) for f in factors], axis=0)
        s = jnp.concatenate([jnp.full((8, LANES), f[1], f32) for f in factors], axis=0)
        return jnp.maximum(jnp.minimum(total * m + s, 0.0), unit)

    def turn_depth(p, odd):
        for c in range(3):
            deep_ref[odd, c] = jnp.dot(
                pieces[c, pl.ds(2 * p, 2)].reshape(256, 4 * LANES), stencils[c],
                preferred_element_type=f32,
            )

    def levels(p, odd):
        for k in range(2):
            for t in range(8):
                lev = level_of(p, odd, k, t)
                high = lev.astype(bf16)
                low = (lev - high.astype(f32)).astype(bf16)
                here = pl.ds(128 * k + 16 * t, 16)
                split[odd, here, pl.ds(0, LANES)] = high
                split[odd, here, pl.ds(LANES, LANES)] = low

    def finish(p, odd):
        turned = lax.dot_general(
            lower[...], split[odd], (((1,), (1,)), ((), ())), preferred_element_type=f32
        )
        first = jnp.zeros((8, 256), f32)
        second = jnp.zeros((8, 256), f32)
        for z in range(16):
            passing = jnp.exp2(turned[8 * z : 8 * z + 8])
            lev = turned[128 + 8 * z : 136 + 8 * z]
            left = passing * jnp.exp2(lev)
            one = (passing - left) * lev
            first = first + one
            second = second + one * lev
        rows = [
            jnp.sum(first, axis=0, keepdims=True),
            jnp.sum(second, axis=0, keepdims=True),
            left[7:8],
        ]
        for q in range(3):
            for k in range(2):
                parts[p // 2, pl.ds(4 * q + 2 * (p % 2) + k, 1)] = rows[q][:, 128 * k : 128 * k + 128]

    def part_copy(b, source):
        return pltpu.make_async_remote_copy(
            src_ref=parts.at[b], dst_ref=arrived.at[source], send_sem=part_send.at[b],
            recv_sem=part_recv.at[source], device_id={"view": b}, device_id_type=MESH,
        )

    def hand_over(b):
        @pl.when(b != v)
        def _():
            part_copy(b, v).start()

        @pl.when(b == v)
        def _():
            arrived[v] = parts[b]

    pl.semaphore_wait(ready, 2)

    turn_depth(1, 1)
    levels(1, 1)

    @pl.loop(1, VIEW - 1)
    def _(b):
        turn_depth(2 * b, 0)
        finish(2 * b - 1, 1)
        levels(2 * b, 0)
        turn_depth(2 * b + 1, 1)
        finish(2 * b, 0)
        levels(2 * b + 1, 1)

        @pl.when(b > 1)
        def _():
            hand_over(b - 1)

    turn_depth(14, 0)
    finish(13, 1)
    levels(14, 0)
    hand_over(6)
    turn_depth(0, 1)
    finish(14, 0)
    turn_depth(15, 0)

    for copy in halos[:2]:
        copy.wait_recv()

    levels(0, 1)
    finish(0, 1)
    hand_over(0)
    levels(15, 0)
    finish(15, 0)
    hand_over(7)

    for step in range(1, VIEW):
        part_copy(view(step), view(step)).wait_recv()

    red = jnp.zeros((ROWS, LANES), f32)
    green = jnp.zeros((ROWS, LANES), f32)
    ahead = jnp.ones((ROWS, LANES), f32)
    for s in range(VIEW):
        red = red + ahead * arrived[s, 0:4]
        green = green + ahead * arrived[s, 4:8]
        ahead = ahead * arrived[s, 8:12]
    red = red * (1.0 / unit)
    green = 4.0 * (red - green * (1.0 / (unit * unit)))
    out[0, 0, 0] = red
    out[0, 0, 1] = green
    out[0, 0, 2] = (1.0 - ahead) - red
    out[0, 0, 3] = 1.0 - ahead

    for copy in halos + z_copies:
        copy.wait_send()
    for step in range(1, VIEW):
        part_copy(view(step), v).wait_send()


def local(velocity, occupied, q_floor, q_span):
    f32, bf16 = jnp.float32, jnp.bfloat16
    here = pl.BlockSpec(memory_space=pltpu.HBM)
    return pl.pallas_call(
        kernel,
        out_shape=jax.ShapeDtypeStruct((1, 1, 4, ROWS, LANES), f32),
        in_specs=[here] * 4,
        out_specs=pl.BlockSpec(memory_space=pltpu.VMEM),
        scratch_shapes=[
            pltpu.VMEM((3, 36, 144, LANES), f32),
            pltpu.VMEM((3, 32, 128, 4 * LANES), bf16),
            pltpu.VMEM((3, 4 * LANES, LANES), bf16),
            pltpu.VMEM((2, 128, LANES), f32),
            pltpu.VMEM((2, 128, LANES), f32),
            pltpu.VMEM((2, 128, LANES), f32),
            pltpu.VMEM((2, 128, LANES), f32),
            pltpu.VMEM((2, 3, 256, LANES), f32),
            pltpu.VMEM((2, 256, 256), bf16),
            pltpu.VMEM((256, 256), bf16),
            pltpu.VMEM((VIEW, 16, LANES), f32),
            pltpu.VMEM((VIEW, 16, LANES), f32),
            pltpu.SemaphoreType.DMA((2, 3)),
            pltpu.SemaphoreType.DMA((4,)),
            pltpu.SemaphoreType.DMA((4,)),
            pltpu.SemaphoreType.DMA((2, 2)),
            pltpu.SemaphoreType.DMA((2, 2)),
            pltpu.SemaphoreType.DMA((VIEW,)),
            pltpu.SemaphoreType.DMA((VIEW,)),
            pltpu.SemaphoreType.REGULAR,
            pltpu.SMEM((4, 1, 16), jnp.int32),
            pltpu.SMEM((1, 1), f32),
            pltpu.SMEM((1, 1), f32),
            pltpu.SemaphoreType.DMA((3,)),
        ],
        compiler_params=pltpu.CompilerParams(collective_id=0, has_side_effects=True),
    )(velocity, occupied.transpose(0, 2, 1), q_floor.reshape(1, 1), q_span.reshape(1, 1))


def solution(mesh):
    placed = (P(None, "gx", "gy", "view"), P("gx", "gy", "view"), P(), P())
    return jax.shard_map(
        local,
        mesh=mesh,
        in_specs=placed,
        out_specs=P("gx", "gy", None, "view", None),
        check_vma=False,
    )
```

```python
import functools
import math

import jax
import jax.numpy as jnp
from jax import lax
from jax.experimental import pallas as pl
from jax.experimental.pallas import tpu as pltpu
from jax.sharding import PartitionSpec as P

MESH = pl.DeviceIdType.MESH
SUB = 8
LANES = 128
ROWS = 4
VIEW = 8
CHUNKS = 4
CUT = 128 // CHUNKS


def stencil(a, b, c, d):
    return (c - b) - 0.125 * (d - a)


def kernel(
    vel, occ_in, q_floor_in, q_span_in, out,
    cells, pieces, stencils, send_l, send_r, recv_l, recv_r, deep_ref, split, lower, parts, arrived,
    load_sem, halo_send, halo_recv, z_send, z_recv, part_send, part_recv, ready,
    occ, q_floor, q_span, small_sem,
):
    f32, bf16 = jnp.float32, jnp.bfloat16
    v = lax.axis_index("view")
    gx = lax.axis_index("gx")
    gy = lax.axis_index("gy")
    n_gx, n_gy = lax.axis_size("gx"), lax.axis_size("gy")

    def view(step):
        return lax.rem(v + VIEW + step, VIEW)

    x_next, x_prev = lax.rem(gx + 1, n_gx), lax.rem(gx + n_gx - 1, n_gx)
    y_next, y_prev = lax.rem(gy + 1, n_gy), lax.rem(gy + n_gy - 1, n_gy)

    loads = []
    for j in range(CHUNKS):
        for c in range(3):
            load = pltpu.make_async_copy(
                vel.at[c, :, pl.ds(CUT * j, CUT)],
                cells.at[c, pl.ds(2, 32), pl.ds(8 + CUT * j, CUT)],
                load_sem.at[j, c],
            )
            load.start()
            loads.append(load)

    small = []
    for n, (src, dst) in enumerate(((occ_in, occ), (q_floor_in, q_floor), (q_span_in, q_span))):
        copy = pltpu.make_async_copy(src, dst, small_sem.at[n])
        copy.start()
        small.append(copy)

    barrier = pltpu.get_barrier_semaphore()
    for target in (
        {"gx": x_next}, {"gx": x_prev}, {"gy": y_next}, {"gy": y_prev},
        {"view": view(1)}, {"view": view(-1)},
    ):
        pl.semaphore_signal(barrier, inc=1, device_id=target, device_id_type=MESH)

    row_id = lax.broadcasted_iota(jnp.int32, (256, 256), 0)
    col_id = lax.broadcasted_iota(jnp.int32, (256, 256), 1)
    depth_of = col_id % LANES
    chosen = ((row_id < LANES) & (depth_of < row_id)) | (depth_of == row_id - LANES)
    lower[...] = chosen.astype(f32).astype(bf16)

    to = lax.broadcasted_iota(jnp.int32, (LANES, LANES), 1)
    row = lax.broadcasted_iota(jnp.int32, (LANES, LANES), 0)

    def weight(gap):
        near = (gap == 1).astype(f32) - (gap == -1).astype(f32)
        far = (gap == 2).astype(f32) - (gap == -2).astype(f32)
        return (near - 0.125 * far).astype(bf16)

    own_weight = weight(row - to)
    halo_at = jnp.where(row % 4 < 2, row % 4 - 2, row % 4 + LANES - 2)
    halo_weight = weight(halo_at - to)
    for c in range(3):
        for n in range(3):
            stencils[c, pl.ds(LANES * n, LANES)] = own_weight
        stencils[c, pl.ds(3 * LANES, LANES)] = jnp.where(
            row // 8 == c, halo_weight, jnp.zeros_like(halo_weight)
        )

    lane = lax.broadcasted_iota(jnp.int32, (16, LANES), 1)
    pair_of = (lane % 8) // 2

    def pack(j):
        @pl.loop(0, CUT // 8)
        def _(q):
            g, t = q % 2, q // 2
            rows = pl.ds(pl.multiple_of(8 + CUT * j + 16 * t, 8), 16)
            own = pl.ds(pl.multiple_of(CUT * j + 16 * t, 16), 16)
            gathered = [jnp.zeros((16, LANES), f32) for s in range(4)]
            for k in range(4):
                for c in range(3):
                    here = lane // 8 == 4 * k + c
                    for s in range(4):
                        u = cells[c, 2 + 16 * g + 4 * s + k, rows]
                        moved = pltpu.roll(u, (32 * k + 8 * c + 4) % LANES, 1)
                        gathered[s] = jnp.where(here, moved, gathered[s])
            left = right = None
            for s in range(4):
                turned = gathered[s] if s == 2 else pltpu.roll(gathered[s], (2 * s - 4) % LANES, 1)
                left = turned if s == 0 else jnp.where(pair_of == s, turned, left)
                right = turned if s == 0 else jnp.where(pair_of == (s + 3) % 4, turned, right)
            send_l[g, own] = left
            send_r[g, own] = right

    halos = []

    def enter():
        pl.semaphore_wait(barrier, 6)


        def send_halo(number, src, dst, target):
            copy = pltpu.make_async_remote_copy(
                src_ref=src, dst_ref=dst, send_sem=halo_send.at[number], recv_sem=halo_recv.at[number],
                device_id=target, device_id_type=MESH,
            )
            copy.start()
            halos.append(copy)

        body = pl.ds(8, 128)
        send_halo(0, vel.at[:, pl.ds(0, 2)], cells.at[:, pl.ds(34, 2), body], {"gx": x_prev})
        send_halo(1, vel.at[:, pl.ds(30, 2)], cells.at[:, pl.ds(0, 2), body], {"gx": x_next})
        send_halo(2, vel.at[:, :, pl.ds(0, 2)], cells.at[:, pl.ds(2, 32), pl.ds(136, 2)], {"gy": y_prev})
        send_halo(3, vel.at[:, :, pl.ds(126, 2)], cells.at[:, pl.ds(2, 32), pl.ds(6, 2)], {"gy": y_next})

    z_copies = []
    for j in range(CHUNKS):
        for c in range(3):
            loads[3 * j + c].wait()
        pack(j)
        if j == 0:
            enter()
        part = pl.ds(CUT * j, CUT)
        for side, (src, dst, step) in enumerate(((send_l, recv_l, -1), (send_r, recv_r, 1))):
            copy = pltpu.make_async_remote_copy(
                src_ref=src.at[:, part], dst_ref=dst.at[:, part], send_sem=z_send.at[j, side],
                recv_sem=z_recv.at[j, side], device_id={"view": view(step)}, device_id_type=MESH,
            )
            copy.start()
            z_copies.append(copy)

    @pl.loop(0, 32)
    def _(x):
        for c in range(3):
            for t in range(8):
                own = pl.ds(16 * t, 16)
                u = cells[c, 2 + x, pl.ds(8 + 16 * t, 16)]
                high = u.astype(bf16)
                rest = u - high.astype(f32)
                mid = rest.astype(bf16)
                low = (rest - mid.astype(f32)).astype(bf16)
                pieces[c, x, own, pl.ds(0, LANES)] = high
                pieces[c, x, own, pl.ds(LANES, LANES)] = mid
                pieces[c, x, own, pl.ds(2 * LANES, LANES)] = low

    for j in range(CHUNKS):
        for copy in z_copies[2 * j : 2 * j + 2]:
            copy.wait_recv()
        if j == 0:
            for step in (2, -2):
                pl.semaphore_signal(
                    ready, inc=1, device_id={"view": view(step)}, device_id_type=MESH
                )

        @pl.loop(0, CUT // 8)
        def _(q):
            g, t = q % 2, q // 2
            own = pl.ds(pl.multiple_of(CUT * j + 16 * t, 16), 16)
            after, before = recv_l[g, own], recv_r[g, own]
            for s in range(4):
                both = jnp.where(pair_of == s, after, before)
                high = both.astype(bf16).astype(f32)
                rest = pltpu.roll(both - high, 4, 1)
                used = (pair_of == s) | (pair_of == (s + 3) % 4)
                halo = jnp.where(used, high, rest)
                for k in range(4):
                    placed = pltpu.roll(halo, (2 - 32 * k - 2 * s) % LANES, 1).astype(bf16)
                    for c in range(3):
                        pieces[c, 16 * g + 4 * s + k, own, pl.ds(3 * LANES, LANES)] = placed

    for copy in halos[2:]:
        copy.wait_recv()

    for copy in small:
        copy.wait()

    unit = -(5.0 / (LANES * VIEW)) * math.log2(math.e)
    slope = -unit / (4.5 * q_span[0, 0])
    shift = -unit * q_floor[0, 0] / q_span[0, 0]

    def level_of(p, odd, k, t):
        x = 2 * p + k + 2
        top = 8 + 16 * t
        grad = []
        for c in range(3):
            def at(dx, dy):
                return cells[c, x + dx, pl.ds(top + dy, 16)]

            across = stencil(at(-2, 0), at(-1, 0), at(1, 0), at(2, 0))
            down = stencil(at(0, -2), at(0, -1), at(0, 1), at(0, 2))
            deep = deep_ref[odd, c, pl.ds(128 * k + 16 * t, 16)]
            grad.append((across, down, deep))
        squares = grad[0][0] * grad[0][0] + grad[1][1] * grad[1][1] + grad[2][2] * grad[2][2]
        cross = grad[0][1] * grad[1][0] + grad[0][2] * grad[2][0] + grad[1][2] * grad[2][1]
        total = (squares + cross) + cross
        factors = []
        for half in range(2):
            keep = occ[p // 4, 0, 2 * t + half].astype(f32)
            factors.append((slope * keep, shift * keep))
        m = jnp.concatenate([jnp.full((8, LANES), f[0], f32) for f in factors], axis=0)
        s = jnp.concatenate([jnp.full((8, LANES), f[1], f32) for f in factors], axis=0)
        return jnp.maximum(jnp.minimum(total * m + s, 0.0), unit)

    def turn_depth(p, odd):
        for c in range(3):
            deep_ref[odd, c] = jnp.dot(
                pieces[c, pl.ds(2 * p, 2)].reshape(256, 4 * LANES), stencils[c],
                preferred_element_type=f32,
            )

    def levels(p, odd):
        for k in range(2):
            for t in range(8):
                lev = level_of(p, odd, k, t)
                high = lev.astype(bf16)
                low = (lev - high.astype(f32)).astype(bf16)
                here = pl.ds(128 * k + 16 * t, 16)
                split[odd, here, pl.ds(0, LANES)] = high
                split[odd, here, pl.ds(LANES, LANES)] = low

    def finish(p, odd):
        turned = lax.dot_general(
            lower[...], split[odd], (((1,), (1,)), ((), ())), preferred_element_type=f32
        )
        first = jnp.zeros((8, 256), f32)
        second = jnp.zeros((8, 256), f32)
        for z in range(16):
            passing = jnp.exp2(turned[8 * z : 8 * z + 8])
            lev = turned[128 + 8 * z : 136 + 8 * z]
            left = passing * jnp.exp2(lev)
            one = (passing - left) * lev
            first = first + one
            second = second + one * lev
        rows = [
            jnp.sum(first, axis=0, keepdims=True),
            jnp.sum(second, axis=0, keepdims=True),
            left[7:8],
        ]
        for q in range(3):
            for k in range(2):
                parts[p // 2, pl.ds(4 * q + 2 * (p % 2) + k, 1)] = rows[q][:, 128 * k : 128 * k + 128]

    def part_copy(b, source):
        return pltpu.make_async_remote_copy(
            src_ref=parts.at[b], dst_ref=arrived.at[source], send_sem=part_send.at[b],
            recv_sem=part_recv.at[source], device_id={"view": b}, device_id_type=MESH,
        )

    def hand_over(b):
        @pl.when(b != v)
        def _():
            part_copy(b, v).start()

        @pl.when(b == v)
        def _():
            arrived[v] = parts[b]

    turn_depth(1, 1)
    levels(1, 1)

    @pl.loop(1, VIEW - 1)
    def _(b):
        turn_depth(2 * b, 0)
        finish(2 * b - 1, 1)
        levels(2 * b, 0)
        turn_depth(2 * b + 1, 1)
        finish(2 * b, 0)
        levels(2 * b + 1, 1)

        @pl.when(b == 2)
        def _():
            pl.semaphore_wait(ready, 2)

        @pl.when(b > 1)
        def _():
            hand_over(b - 1)

    turn_depth(14, 0)
    finish(13, 1)
    levels(14, 0)
    hand_over(6)
    turn_depth(0, 1)
    finish(14, 0)
    turn_depth(15, 0)

    for copy in halos[:2]:
        copy.wait_recv()

    levels(0, 1)
    finish(0, 1)
    hand_over(0)
    levels(15, 0)
    finish(15, 0)
    hand_over(7)

    for step in range(1, VIEW):
        part_copy(view(step), view(step)).wait_recv()

    red = jnp.zeros((ROWS, LANES), f32)
    green = jnp.zeros((ROWS, LANES), f32)
    ahead = jnp.ones((ROWS, LANES), f32)
    for s in range(VIEW):
        red = red + ahead * arrived[s, 0:4]
        green = green + ahead * arrived[s, 4:8]
        ahead = ahead * arrived[s, 8:12]
    red = red * (1.0 / unit)
    green = 4.0 * (red - green * (1.0 / (unit * unit)))
    out[0, 0, 0] = red
    out[0, 0, 1] = green
    out[0, 0, 2] = (1.0 - ahead) - red
    out[0, 0, 3] = 1.0 - ahead

    for copy in halos + z_copies:
        copy.wait_send()
    for step in range(1, VIEW):
        part_copy(view(step), v).wait_send()


def local(velocity, occupied, q_floor, q_span):
    f32, bf16 = jnp.float32, jnp.bfloat16
    here = pl.BlockSpec(memory_space=pltpu.HBM)
    return pl.pallas_call(
        kernel,
        out_shape=jax.ShapeDtypeStruct((1, 1, 4, ROWS, LANES), f32),
        in_specs=[here] * 4,
        out_specs=pl.BlockSpec(memory_space=pltpu.VMEM),
        scratch_shapes=[
            pltpu.VMEM((3, 36, 144, LANES), f32),
            pltpu.VMEM((3, 32, 128, 4 * LANES), bf16),
            pltpu.VMEM((3, 4 * LANES, LANES), bf16),
            pltpu.VMEM((2, 128, LANES), f32),
            pltpu.VMEM((2, 128, LANES), f32),
            pltpu.VMEM((2, 128, LANES), f32),
            pltpu.VMEM((2, 128, LANES), f32),
            pltpu.VMEM((2, 3, 256, LANES), f32),
            pltpu.VMEM((2, 256, 256), bf16),
            pltpu.VMEM((256, 256), bf16),
            pltpu.VMEM((VIEW, 16, LANES), f32),
            pltpu.VMEM((VIEW, 16, LANES), f32),
            pltpu.SemaphoreType.DMA((CHUNKS, 3)),
            pltpu.SemaphoreType.DMA((4,)),
            pltpu.SemaphoreType.DMA((4,)),
            pltpu.SemaphoreType.DMA((CHUNKS, 2)),
            pltpu.SemaphoreType.DMA((CHUNKS, 2)),
            pltpu.SemaphoreType.DMA((VIEW,)),
            pltpu.SemaphoreType.DMA((VIEW,)),
            pltpu.SemaphoreType.REGULAR,
            pltpu.SMEM((4, 1, 16), jnp.int32),
            pltpu.SMEM((1, 1), f32),
            pltpu.SMEM((1, 1), f32),
            pltpu.SemaphoreType.DMA((3,)),
        ],
        compiler_params=pltpu.CompilerParams(collective_id=0, has_side_effects=True),
    )(velocity, occupied.transpose(0, 2, 1), q_floor.reshape(1, 1), q_span.reshape(1, 1))


def solution(mesh):
    placed = (P(None, "gx", "gy", "view"), P("gx", "gy", "view"), P(), P())
    return jax.shard_map(
        local,
        mesh=mesh,
        in_specs=placed,
        out_specs=P("gx", "gy", None, "view", None),
        check_vma=False,
    )
```

```python
import functools
import math

import jax
import jax.numpy as jnp
from jax import lax
from jax.experimental import pallas as pl
from jax.experimental.pallas import tpu as pltpu
from jax.sharding import PartitionSpec as P

MESH = pl.DeviceIdType.MESH
SUB = 8
LANES = 128
ROWS = 4
VIEW = 8
CHUNKS = 4
CUT = 128 // CHUNKS


def stencil(a, b, c, d):
    return (c - b) - 0.125 * (d - a)


def kernel(
    vel, occ_in, q_floor_in, q_span_in, out,
    cells, pieces, stencils, send_l, send_r, recv_l, recv_r, deep_ref, split, lower, parts, arrived,
    load_sem, halo_send, halo_recv, z_send, z_recv, part_send, part_recv, ready,
    occ, q_floor, q_span, small_sem,
):
    f32, bf16 = jnp.float32, jnp.bfloat16
    v = lax.axis_index("view")
    gx = lax.axis_index("gx")
    gy = lax.axis_index("gy")
    n_gx, n_gy = lax.axis_size("gx"), lax.axis_size("gy")

    def view(step):
        return lax.rem(v + VIEW + step, VIEW)

    x_next, x_prev = lax.rem(gx + 1, n_gx), lax.rem(gx + n_gx - 1, n_gx)
    y_next, y_prev = lax.rem(gy + 1, n_gy), lax.rem(gy + n_gy - 1, n_gy)

    loads = []
    for j in range(CHUNKS):
        for c in range(3):
            load = pltpu.make_async_copy(
                vel.at[c, :, pl.ds(CUT * j, CUT)],
                cells.at[c, pl.ds(2, 32), pl.ds(8 + CUT * j, CUT)],
                load_sem.at[j, c],
            )
            load.start()
            loads.append(load)

    small = []
    for n, (src, dst) in enumerate(((occ_in, occ), (q_floor_in, q_floor), (q_span_in, q_span))):
        copy = pltpu.make_async_copy(src, dst, small_sem.at[n])
        copy.start()
        small.append(copy)

    barrier = pltpu.get_barrier_semaphore()
    for target in (
        {"gx": x_next}, {"gx": x_prev}, {"gy": y_next}, {"gy": y_prev},
        {"view": view(1)}, {"view": view(-1)},
    ):
        pl.semaphore_signal(barrier, inc=1, device_id=target, device_id_type=MESH)

    row_id = lax.broadcasted_iota(jnp.int32, (256, 256), 0)
    col_id = lax.broadcasted_iota(jnp.int32, (256, 256), 1)
    depth_of = col_id % LANES
    chosen = ((row_id < LANES) & (depth_of < row_id)) | (depth_of == row_id - LANES)
    lower[...] = chosen.astype(f32).astype(bf16)

    to = lax.broadcasted_iota(jnp.int32, (LANES, LANES), 1)
    row = lax.broadcasted_iota(jnp.int32, (LANES, LANES), 0)

    def weight(gap):
        near = (gap == 1).astype(f32) - (gap == -1).astype(f32)
        far = (gap == 2).astype(f32) - (gap == -2).astype(f32)
        return (near - 0.125 * far).astype(bf16)

    own_weight = weight(row - to)
    halo_at = jnp.where(row % 4 < 2, row % 4 - 2, row % 4 + LANES - 2)
    halo_weight = weight(halo_at - to)
    for c in range(3):
        for n in range(3):
            stencils[c, pl.ds(LANES * n, LANES)] = own_weight
        stencils[c, pl.ds(3 * LANES, LANES)] = jnp.where(
            row // 8 == c, halo_weight, jnp.zeros_like(halo_weight)
        )

    lane = lax.broadcasted_iota(jnp.int32, (16, LANES), 1)
    pair_of = (lane % 8) // 2

    def pack(j):
        @pl.loop(0, CUT // 16)
        def _(t):
            rows = pl.ds(pl.multiple_of(8 + CUT * j + 16 * t, 8), 16)
            own = pl.ds(pl.multiple_of(CUT * j + 16 * t, 16), 16)
            for g in range(2):
                gathered = [jnp.zeros((16, LANES), f32) for s in range(4)]
                for k in range(4):
                    for c in range(3):
                        here = lane // 8 == 4 * k + c
                        for s in range(4):
                            u = cells[c, 2 + 16 * g + 4 * s + k, rows]
                            moved = pltpu.roll(u, (32 * k + 8 * c + 4) % LANES, 1)
                            gathered[s] = jnp.where(here, moved, gathered[s])
                left = right = None
                for s in range(4):
                    turned = gathered[s] if s == 2 else pltpu.roll(gathered[s], (2 * s - 4) % LANES, 1)
                    left = turned if s == 0 else jnp.where(pair_of == s, turned, left)
                    right = turned if s == 0 else jnp.where(pair_of == (s + 3) % 4, turned, right)
                send_l[g, own] = left
                send_r[g, own] = right

    halos = []

    def enter():
        pl.semaphore_wait(barrier, 6)


        def send_halo(number, src, dst, target):
            copy = pltpu.make_async_remote_copy(
                src_ref=src, dst_ref=dst, send_sem=halo_send.at[number], recv_sem=halo_recv.at[number],
                device_id=target, device_id_type=MESH,
            )
            copy.start()
            halos.append(copy)

        body = pl.ds(8, 128)
        send_halo(0, vel.at[:, pl.ds(30, 2)], cells.at[:, pl.ds(0, 2), body], {"gx": x_next})
        send_halo(1, vel.at[:, pl.ds(0, 2)], cells.at[:, pl.ds(34, 2), body], {"gx": x_prev})
        send_halo(2, vel.at[:, :, pl.ds(0, 2)], cells.at[:, pl.ds(2, 32), pl.ds(136, 2)], {"gy": y_prev})
        send_halo(3, vel.at[:, :, pl.ds(126, 2)], cells.at[:, pl.ds(2, 32), pl.ds(6, 2)], {"gy": y_next})

    enter()

    z_copies = []
    for j in range(CHUNKS):
        for c in range(3):
            loads[3 * j + c].wait()
        pack(j)
        part = pl.ds(CUT * j, CUT)
        for side, (src, dst, step) in enumerate(((send_l, recv_l, -1), (send_r, recv_r, 1))):
            copy = pltpu.make_async_remote_copy(
                src_ref=src.at[:, part], dst_ref=dst.at[:, part], send_sem=z_send.at[j, side],
                recv_sem=z_recv.at[j, side], device_id={"view": view(step)}, device_id_type=MESH,
            )
            copy.start()
            z_copies.append(copy)

    @pl.loop(0, 32)
    def _(x):
        for c in range(3):
            for t in range(8):
                own = pl.ds(16 * t, 16)
                u = cells[c, 2 + x, pl.ds(8 + 16 * t, 16)]
                high = u.astype(bf16)
                rest = u - high.astype(f32)
                mid = rest.astype(bf16)
                low = (rest - mid.astype(f32)).astype(bf16)
                pieces[c, x, own, pl.ds(0, LANES)] = high
                pieces[c, x, own, pl.ds(LANES, LANES)] = mid
                pieces[c, x, own, pl.ds(2 * LANES, LANES)] = low

    for j in range(CHUNKS):
        for copy in z_copies[2 * j : 2 * j + 2]:
            copy.wait_recv()
        if j == 0:
            for step in (2, -2):
                pl.semaphore_signal(
                    ready, inc=1, device_id={"view": view(step)}, device_id_type=MESH
                )

        @pl.loop(0, CUT // 8)
        def _(q):
            g, t = q % 2, q // 2
            own = pl.ds(pl.multiple_of(CUT * j + 16 * t, 16), 16)
            after, before = recv_l[g, own], recv_r[g, own]
            for s in range(4):
                both = jnp.where(pair_of == s, after, before)
                high = both.astype(bf16).astype(f32)
                rest = pltpu.roll(both - high, 4, 1)
                used = (pair_of == s) | (pair_of == (s + 3) % 4)
                halo = jnp.where(used, high, rest)
                for k in range(4):
                    placed = pltpu.roll(halo, (2 - 32 * k - 2 * s) % LANES, 1).astype(bf16)
                    for c in range(3):
                        pieces[c, 16 * g + 4 * s + k, own, pl.ds(3 * LANES, LANES)] = placed

    for copy in halos[2:]:
        copy.wait_recv()

    for copy in small:
        copy.wait()

    unit = -(5.0 / (LANES * VIEW)) * math.log2(math.e)
    slope = -unit / (4.5 * q_span[0, 0])
    shift = -unit * q_floor[0, 0] / q_span[0, 0]

    def level_of(p, odd, k, t):
        x = 2 * p + k + 2
        top = 8 + 16 * t
        grad = []
        for c in range(3):
            def at(dx, dy):
                return cells[c, x + dx, pl.ds(top + dy, 16)]

            across = stencil(at(-2, 0), at(-1, 0), at(1, 0), at(2, 0))
            down = stencil(at(0, -2), at(0, -1), at(0, 1), at(0, 2))
            deep = deep_ref[odd, c, pl.ds(128 * k + 16 * t, 16)]
            grad.append((across, down, deep))
        squares = grad[0][0] * grad[0][0] + grad[1][1] * grad[1][1] + grad[2][2] * grad[2][2]
        cross = grad[0][1] * grad[1][0] + grad[0][2] * grad[2][0] + grad[1][2] * grad[2][1]
        total = (squares + cross) + cross
        factors = []
        for half in range(2):
            keep = occ[p // 4, 0, 2 * t + half].astype(f32)
            factors.append((slope * keep, shift * keep))
        m = jnp.concatenate([jnp.full((8, LANES), f[0], f32) for f in factors], axis=0)
        s = jnp.concatenate([jnp.full((8, LANES), f[1], f32) for f in factors], axis=0)
        return jnp.maximum(jnp.minimum(total * m + s, 0.0), unit)

    def turn_depth(p, odd):
        for c in range(3):
            deep_ref[odd, c] = jnp.dot(
                pieces[c, pl.ds(2 * p, 2)].reshape(256, 4 * LANES), stencils[c],
                preferred_element_type=f32,
            )

    def levels(p, odd):
        for k in range(2):
            for t in range(8):
                lev = level_of(p, odd, k, t)
                high = lev.astype(bf16)
                low = (lev - high.astype(f32)).astype(bf16)
                here = pl.ds(128 * k + 16 * t, 16)
                split[odd, here, pl.ds(0, LANES)] = high
                split[odd, here, pl.ds(LANES, LANES)] = low

    def finish(p, odd):
        turned = lax.dot_general(
            lower[...], split[odd], (((1,), (1,)), ((), ())), preferred_element_type=f32
        )
        first = jnp.zeros((8, 256), f32)
        second = jnp.zeros((8, 256), f32)
        for z in range(16):
            passing = jnp.exp2(turned[8 * z : 8 * z + 8])
            lev = turned[128 + 8 * z : 136 + 8 * z]
            left = passing * jnp.exp2(lev)
            one = (passing - left) * lev
            first = first + one
            second = second + one * lev
        rows = [
            jnp.sum(first, axis=0, keepdims=True),
            jnp.sum(second, axis=0, keepdims=True),
            left[7:8],
        ]
        for q in range(3):
            for k in range(2):
                parts[p // 2, pl.ds(4 * q + 2 * (p % 2) + k, 1)] = rows[q][:, 128 * k : 128 * k + 128]

    def part_copy(b, source):
        return pltpu.make_async_remote_copy(
            src_ref=parts.at[b], dst_ref=arrived.at[source], send_sem=part_send.at[b],
            recv_sem=part_recv.at[source], device_id={"view": b}, device_id_type=MESH,
        )

    def hand_over(b):
        @pl.when(b != v)
        def _():
            part_copy(b, v).start()

        @pl.when(b == v)
        def _():
            arrived[v] = parts[b]

    turn_depth(1, 1)
    levels(1, 1)

    @pl.loop(1, VIEW - 2)
    def _(b):
        turn_depth(2 * b, 0)
        finish(2 * b - 1, 1)
        levels(2 * b, 0)
        turn_depth(2 * b + 1, 1)
        finish(2 * b, 0)
        levels(2 * b + 1, 1)

        @pl.when(b == 2)
        def _():
            pl.semaphore_wait(ready, 2)

        @pl.when(b > 1)
        def _():
            hand_over(b - 1)

    turn_depth(0, 0)
    finish(11, 1)
    hand_over(5)

    halos[0].wait_recv()
    levels(0, 0)
    finish(0, 0)
    hand_over(0)

    turn_depth(12, 1)
    levels(12, 1)
    turn_depth(13, 0)
    finish(12, 1)
    levels(13, 0)
    turn_depth(14, 1)
    finish(13, 0)
    hand_over(6)
    levels(14, 1)
    turn_depth(15, 0)
    finish(14, 1)

    halos[1].wait_recv()
    levels(15, 0)
    finish(15, 0)
    hand_over(7)

    for step in range(1, VIEW):
        part_copy(view(step), view(step)).wait_recv()

    red = jnp.zeros((ROWS, LANES), f32)
    green = jnp.zeros((ROWS, LANES), f32)
    ahead = jnp.ones((ROWS, LANES), f32)
    for s in range(VIEW):
        red = red + ahead * arrived[s, 0:4]
        green = green + ahead * arrived[s, 4:8]
        ahead = ahead * arrived[s, 8:12]
    red = red * (1.0 / unit)
    green = 4.0 * (red - green * (1.0 / (unit * unit)))
    out[0, 0, 0] = red
    out[0, 0, 1] = green
    out[0, 0, 2] = (1.0 - ahead) - red
    out[0, 0, 3] = 1.0 - ahead

    for copy in halos + z_copies:
        copy.wait_send()
    for step in range(1, VIEW):
        part_copy(view(step), v).wait_send()


def local(velocity, occupied, q_floor, q_span):
    f32, bf16 = jnp.float32, jnp.bfloat16
    here = pl.BlockSpec(memory_space=pltpu.HBM)
    return pl.pallas_call(
        kernel,
        out_shape=jax.ShapeDtypeStruct((1, 1, 4, ROWS, LANES), f32),
        in_specs=[here] * 4,
        out_specs=pl.BlockSpec(memory_space=pltpu.VMEM),
        scratch_shapes=[
            pltpu.VMEM((3, 36, 144, LANES), f32),
            pltpu.VMEM((3, 32, 128, 4 * LANES), bf16),
            pltpu.VMEM((3, 4 * LANES, LANES), bf16),
            pltpu.VMEM((2, 128, LANES), f32),
            pltpu.VMEM((2, 128, LANES), f32),
            pltpu.VMEM((2, 128, LANES), f32),
            pltpu.VMEM((2, 128, LANES), f32),
            pltpu.VMEM((2, 3, 256, LANES), f32),
            pltpu.VMEM((2, 256, 256), bf16),
            pltpu.VMEM((256, 256), bf16),
            pltpu.VMEM((VIEW, 16, LANES), f32),
            pltpu.VMEM((VIEW, 16, LANES), f32),
            pltpu.SemaphoreType.DMA((CHUNKS, 3)),
            pltpu.SemaphoreType.DMA((4,)),
            pltpu.SemaphoreType.DMA((4,)),
            pltpu.SemaphoreType.DMA((CHUNKS, 2)),
            pltpu.SemaphoreType.DMA((CHUNKS, 2)),
            pltpu.SemaphoreType.DMA((VIEW,)),
            pltpu.SemaphoreType.DMA((VIEW,)),
            pltpu.SemaphoreType.REGULAR,
            pltpu.SMEM((4, 1, 16), jnp.int32),
            pltpu.SMEM((1, 1), f32),
            pltpu.SMEM((1, 1), f32),
            pltpu.SemaphoreType.DMA((3,)),
        ],
        compiler_params=pltpu.CompilerParams(collective_id=0, has_side_effects=True),
    )(velocity, occupied.transpose(0, 2, 1), q_floor.reshape(1, 1), q_span.reshape(1, 1))


def solution(mesh):
    placed = (P(None, "gx", "gy", "view"), P("gx", "gy", "view"), P(), P())
    return jax.shard_map(
        local,
        mesh=mesh,
        in_specs=placed,
        out_specs=P("gx", "gy", None, "view", None),
        check_vma=False,
    )
```

```python
import functools
import math

import jax
import jax.numpy as jnp
from jax import lax
from jax.experimental import pallas as pl
from jax.experimental.pallas import tpu as pltpu
from jax.sharding import PartitionSpec as P

MESH = pl.DeviceIdType.MESH
SUB = 8
LANES = 128
ROWS = 4
VIEW = 8
CHUNKS = 4
CUT = 128 // CHUNKS


def stencil(a, b, c, d):
    return (c - b) - 0.125 * (d - a)


def kernel(
    vel, occ_in, q_floor_in, q_span_in, out,
    cells, pieces, stencils, send_l, send_r, recv_l, recv_r, deep_ref, split, lower, parts, arrived,
    load_sem, halo_send, halo_recv, z_send, z_recv, part_send, part_recv, ready,
    occ, q_floor, q_span, small_sem,
):
    f32, bf16 = jnp.float32, jnp.bfloat16
    v = lax.axis_index("view")
    gx = lax.axis_index("gx")
    gy = lax.axis_index("gy")
    n_gx, n_gy = lax.axis_size("gx"), lax.axis_size("gy")

    def view(step):
        return lax.rem(v + VIEW + step, VIEW)

    x_next, x_prev = lax.rem(gx + 1, n_gx), lax.rem(gx + n_gx - 1, n_gx)
    y_next, y_prev = lax.rem(gy + 1, n_gy), lax.rem(gy + n_gy - 1, n_gy)

    barrier = pltpu.get_barrier_semaphore()
    for target in (
        {"gx": x_next}, {"gx": x_prev}, {"gy": y_next}, {"gy": y_prev},
        {"view": view(1)}, {"view": view(-1)},
    ):
        pl.semaphore_signal(barrier, inc=1, device_id=target, device_id_type=MESH)

    loads = []
    for j in range(CHUNKS):
        for c in range(3):
            load = pltpu.make_async_copy(
                vel.at[c, :, pl.ds(CUT * j, CUT)],
                cells.at[c, pl.ds(2, 32), pl.ds(8 + CUT * j, CUT)],
                load_sem.at[j, c],
            )
            load.start()
            loads.append(load)

    small = []
    for n, (src, dst) in enumerate(((occ_in, occ), (q_floor_in, q_floor), (q_span_in, q_span))):
        copy = pltpu.make_async_copy(src, dst, small_sem.at[n])
        copy.start()
        small.append(copy)

    row_id = lax.broadcasted_iota(jnp.int32, (256, 256), 0)
    col_id = lax.broadcasted_iota(jnp.int32, (256, 256), 1)
    depth_of = col_id % LANES
    chosen = ((row_id < LANES) & (depth_of < row_id)) | (depth_of == row_id - LANES)
    lower[...] = chosen.astype(f32).astype(bf16)

    to = lax.broadcasted_iota(jnp.int32, (LANES, LANES), 1)
    row = lax.broadcasted_iota(jnp.int32, (LANES, LANES), 0)

    def weight(gap):
        near = (gap == 1).astype(f32) - (gap == -1).astype(f32)
        far = (gap == 2).astype(f32) - (gap == -2).astype(f32)
        return (near - 0.125 * far).astype(bf16)

    own_weight = weight(row - to)
    halo_at = jnp.where(row % 4 < 2, row % 4 - 2, row % 4 + LANES - 2)
    halo_weight = weight(halo_at - to)
    for c in range(3):
        for n in range(3):
            stencils[c, pl.ds(LANES * n, LANES)] = own_weight
        stencils[c, pl.ds(3 * LANES, LANES)] = jnp.where(
            row // 8 == c, halo_weight, jnp.zeros_like(halo_weight)
        )

    lane = lax.broadcasted_iota(jnp.int32, (16, LANES), 1)
    pair_of = (lane % 8) // 2

    def pack(j):
        @pl.loop(0, CUT // 16)
        def _(t):
            rows = pl.ds(pl.multiple_of(8 + CUT * j + 16 * t, 8), 16)
            own = pl.ds(pl.multiple_of(CUT * j + 16 * t, 16), 16)
            for g in range(2):
                gathered = [jnp.zeros((16, LANES), f32) for s in range(4)]
                for k in range(4):
                    for c in range(3):
                        here = lane // 8 == 4 * k + c
                        for s in range(4):
                            u = cells[c, 2 + 16 * g + 4 * s + k, rows]
                            moved = pltpu.roll(u, (32 * k + 8 * c + 4) % LANES, 1)
                            gathered[s] = jnp.where(here, moved, gathered[s])
                left = right = None
                for s in range(4):
                    turned = gathered[s] if s == 2 else pltpu.roll(gathered[s], (2 * s - 4) % LANES, 1)
                    left = turned if s == 0 else jnp.where(pair_of == s, turned, left)
                    right = turned if s == 0 else jnp.where(pair_of == (s + 3) % 4, turned, right)
                send_l[g, own] = left
                send_r[g, own] = right

    halos = []

    def send_halo(number, src, dst, target):
        copy = pltpu.make_async_remote_copy(
            src_ref=src, dst_ref=dst, send_sem=halo_send.at[number], recv_sem=halo_recv.at[number],
            device_id=target, device_id_type=MESH,
        )
        copy.start()
        halos.append(copy)

    def enter():
        pl.semaphore_wait(barrier, 6)


        for n in range(2):
            half = pl.ds(64 * n, 64)
            send_halo(
                n, vel.at[:, pl.ds(30, 2), half],
                cells.at[:, pl.ds(0, 2), pl.ds(8 + 64 * n, 64)], {"gx": x_next},
            )
        send_halo(
            2, vel.at[:, :, pl.ds(0, 2)], cells.at[:, pl.ds(2, 32), pl.ds(136, 2)], {"gy": y_prev}
        )
        send_halo(
            3, vel.at[:, :, pl.ds(126, 2)], cells.at[:, pl.ds(2, 32), pl.ds(6, 2)], {"gy": y_next}
        )

    enter()

    z_copies = []
    for j in range(CHUNKS):
        for c in range(3):
            loads[3 * j + c].wait()
        pack(j)
        part = pl.ds(CUT * j, CUT)
        for side, (src, dst, step) in enumerate(((send_l, recv_l, -1), (send_r, recv_r, 1))):
            copy = pltpu.make_async_remote_copy(
                src_ref=src.at[:, part], dst_ref=dst.at[:, part], send_sem=z_send.at[j, side],
                recv_sem=z_recv.at[j, side], device_id={"view": view(step)}, device_id_type=MESH,
            )
            copy.start()
            z_copies.append(copy)

    @pl.loop(0, 32)
    def _(x):
        for c in range(3):
            for t in range(8):
                own = pl.ds(16 * t, 16)
                u = cells[c, 2 + x, pl.ds(8 + 16 * t, 16)]
                high = u.astype(bf16)
                rest = u - high.astype(f32)
                mid = rest.astype(bf16)
                low = (rest - mid.astype(f32)).astype(bf16)
                pieces[c, x, own, pl.ds(0, LANES)] = high
                pieces[c, x, own, pl.ds(LANES, LANES)] = mid
                pieces[c, x, own, pl.ds(2 * LANES, LANES)] = low

    send_halo(
        4, vel.at[:, pl.ds(0, 2)], cells.at[:, pl.ds(34, 2), pl.ds(8, 128)], {"gx": x_prev}
    )

    for j in range(CHUNKS):
        for copy in z_copies[2 * j : 2 * j + 2]:
            copy.wait_recv()
        if j == 0:
            for step in (2, -2):
                pl.semaphore_signal(
                    ready, inc=1, device_id={"view": view(step)}, device_id_type=MESH
                )

        @pl.loop(0, CUT // 8)
        def _(q):
            g, t = q % 2, q // 2
            own = pl.ds(pl.multiple_of(CUT * j + 16 * t, 16), 16)
            after, before = recv_l[g, own], recv_r[g, own]
            for s in range(4):
                both = jnp.where(pair_of == s, after, before)
                high = both.astype(bf16).astype(f32)
                rest = pltpu.roll(both - high, 4, 1)
                used = (pair_of == s) | (pair_of == (s + 3) % 4)
                halo = jnp.where(used, high, rest)
                for k in range(4):
                    placed = pltpu.roll(halo, (2 - 32 * k - 2 * s) % LANES, 1).astype(bf16)
                    for c in range(3):
                        pieces[c, 16 * g + 4 * s + k, own, pl.ds(3 * LANES, LANES)] = placed

    for copy in halos[2:4]:
        copy.wait_recv()

    for copy in small:
        copy.wait()

    unit = -(5.0 / (LANES * VIEW)) * math.log2(math.e)
    slope = -unit / (4.5 * q_span[0, 0])
    shift = -unit * q_floor[0, 0] / q_span[0, 0]

    def level_of(p, odd, k, t):
        x = 2 * p + k + 2
        top = 8 + 16 * t
        grad = []
        for c in range(3):
            def at(dx, dy):
                return cells[c, x + dx, pl.ds(top + dy, 16)]

            across = stencil(at(-2, 0), at(-1, 0), at(1, 0), at(2, 0))
            down = stencil(at(0, -2), at(0, -1), at(0, 1), at(0, 2))
            deep = deep_ref[odd, c, pl.ds(128 * k + 16 * t, 16)]
            grad.append((across, down, deep))
        squares = grad[0][0] * grad[0][0] + grad[1][1] * grad[1][1] + grad[2][2] * grad[2][2]
        cross = grad[0][1] * grad[1][0] + grad[0][2] * grad[2][0] + grad[1][2] * grad[2][1]
        total = (squares + cross) + cross
        factors = []
        for half in range(2):
            keep = occ[p // 4, 0, 2 * t + half].astype(f32)
            factors.append((slope * keep, shift * keep))
        m = jnp.concatenate([jnp.full((8, LANES), f[0], f32) for f in factors], axis=0)
        s = jnp.concatenate([jnp.full((8, LANES), f[1], f32) for f in factors], axis=0)
        return jnp.maximum(jnp.minimum(total * m + s, 0.0), unit)

    def turn_depth(p, odd):
        for c in range(3):
            deep_ref[odd, c] = jnp.dot(
                pieces[c, pl.ds(2 * p, 2)].reshape(256, 4 * LANES), stencils[c],
                preferred_element_type=f32,
            )

    def levels(p, odd, tiles=range(8)):
        for k in range(2):
            for t in tiles:
                lev = level_of(p, odd, k, t)
                high = lev.astype(bf16)
                low = (lev - high.astype(f32)).astype(bf16)
                here = pl.ds(128 * k + 16 * t, 16)
                split[odd, here, pl.ds(0, LANES)] = high
                split[odd, here, pl.ds(LANES, LANES)] = low

    def finish(p, odd):
        turned = lax.dot_general(
            lower[...], split[odd], (((1,), (1,)), ((), ())), preferred_element_type=f32
        )
        first = jnp.zeros((8, 256), f32)
        second = jnp.zeros((8, 256), f32)
        for z in range(16):
            passing = jnp.exp2(turned[8 * z : 8 * z + 8])
            lev = turned[128 + 8 * z : 136 + 8 * z]
            left = passing * jnp.exp2(lev)
            one = (passing - left) * lev
            first = first + one
            second = second + one * lev
        rows = [
            jnp.sum(first, axis=0, keepdims=True),
            jnp.sum(second, axis=0, keepdims=True),
            left[7:8],
        ]
        for q in range(3):
            for k in range(2):
                parts[p // 2, pl.ds(4 * q + 2 * (p % 2) + k, 1)] = rows[q][:, 128 * k : 128 * k + 128]

    def part_copy(b, source):
        return pltpu.make_async_remote_copy(
            src_ref=parts.at[b], dst_ref=arrived.at[source], send_sem=part_send.at[b],
            recv_sem=part_recv.at[source], device_id={"view": b}, device_id_type=MESH,
        )

    def hand_over(b):
        @pl.when(b != v)
        def _():
            part_copy(b, v).start()

        @pl.when(b == v)
        def _():
            arrived[v] = parts[b]

    def two_pairs(p):
        turn_depth(p, 0)
        finish(p - 1, 1)
        levels(p, 0)
        turn_depth(p + 1, 1)
        finish(p, 0)
        levels(p + 1, 1)

    turn_depth(1, 1)
    levels(1, 1)

    @pl.loop(1, 5)
    def _(b):
        two_pairs(2 * b)

        @pl.when(b == 2)
        def _():
            pl.semaphore_wait(ready, 2)

        @pl.when(b > 1)
        def _():
            hand_over(b - 1)

    turn_depth(0, 0)
    finish(9, 1)
    hand_over(4)

    for n in range(2):
        halos[n].wait_recv()
        levels(0, 0, range(4 * n, 4 * n + 4))
    finish(0, 0)
    hand_over(0)

    turn_depth(10, 1)
    levels(10, 1)

    @pl.loop(5, 7)
    def _(b):
        two_pairs(2 * b + 1)
        hand_over(b)

    turn_depth(15, 0)
    finish(14, 1)
    halos[4].wait_recv()
    levels(15, 0)
    finish(15, 0)
    hand_over(7)

    for step in range(1, VIEW):
        part_copy(view(step), view(step)).wait_recv()

    red = jnp.zeros((ROWS, LANES), f32)
    green = jnp.zeros((ROWS, LANES), f32)
    ahead = jnp.ones((ROWS, LANES), f32)
    for s in range(VIEW):
        red = red + ahead * arrived[s, 0:4]
        green = green + ahead * arrived[s, 4:8]
        ahead = ahead * arrived[s, 8:12]
    red = red * (1.0 / unit)
    green = 4.0 * (red - green * (1.0 / (unit * unit)))
    out[0, 0, 0] = red
    out[0, 0, 1] = green
    out[0, 0, 2] = (1.0 - ahead) - red
    out[0, 0, 3] = 1.0 - ahead

    for copy in halos + z_copies:
        copy.wait_send()
    for step in range(1, VIEW):
        part_copy(view(step), v).wait_send()


def local(velocity, occupied, q_floor, q_span):
    f32, bf16 = jnp.float32, jnp.bfloat16
    here = pl.BlockSpec(memory_space=pltpu.HBM)
    return pl.pallas_call(
        kernel,
        out_shape=jax.ShapeDtypeStruct((1, 1, 4, ROWS, LANES), f32),
        in_specs=[here] * 4,
        out_specs=pl.BlockSpec(memory_space=pltpu.VMEM),
        scratch_shapes=[
            pltpu.VMEM((3, 36, 144, LANES), f32),
            pltpu.VMEM((3, 32, 128, 4 * LANES), bf16),
            pltpu.VMEM((3, 4 * LANES, LANES), bf16),
            pltpu.VMEM((2, 128, LANES), f32),
            pltpu.VMEM((2, 128, LANES), f32),
            pltpu.VMEM((2, 128, LANES), f32),
            pltpu.VMEM((2, 128, LANES), f32),
            pltpu.VMEM((2, 3, 256, LANES), f32),
            pltpu.VMEM((2, 256, 256), bf16),
            pltpu.VMEM((256, 256), bf16),
            pltpu.VMEM((VIEW, 16, LANES), f32),
            pltpu.VMEM((VIEW, 16, LANES), f32),
            pltpu.SemaphoreType.DMA((CHUNKS, 3)),
            pltpu.SemaphoreType.DMA((5,)),
            pltpu.SemaphoreType.DMA((5,)),
            pltpu.SemaphoreType.DMA((CHUNKS, 2)),
            pltpu.SemaphoreType.DMA((CHUNKS, 2)),
            pltpu.SemaphoreType.DMA((VIEW,)),
            pltpu.SemaphoreType.DMA((VIEW,)),
            pltpu.SemaphoreType.REGULAR,
            pltpu.SMEM((4, 1, 16), jnp.int32),
            pltpu.SMEM((1, 1), f32),
            pltpu.SMEM((1, 1), f32),
            pltpu.SemaphoreType.DMA((3,)),
        ],
        compiler_params=pltpu.CompilerParams(collective_id=0, has_side_effects=True),
    )(velocity, occupied.transpose(0, 2, 1), q_floor.reshape(1, 1), q_span.reshape(1, 1))


def solution(mesh):
    placed = (P(None, "gx", "gy", "view"), P("gx", "gy", "view"), P(), P())
    return jax.shard_map(
        local,
        mesh=mesh,
        in_specs=placed,
        out_specs=P("gx", "gy", None, "view", None),
        check_vma=False,
    )
```

```python
import functools
import math

import jax
import jax.numpy as jnp
from jax import lax
from jax.experimental import pallas as pl
from jax.experimental.pallas import tpu as pltpu
from jax.sharding import PartitionSpec as P

MESH = pl.DeviceIdType.MESH
SUB = 8
LANES = 128
ROWS = 4
VIEW = 8
CHUNKS = 4
CUT = 128 // CHUNKS


def stencil(a, b, c, d):
    return (c - b) - 0.125 * (d - a)


def kernel(
    vel, occ_in, q_floor_in, q_span_in, out,
    cells, pieces, stencils, send_l, send_r, recv_l, recv_r, deep_ref, split, lower, parts, arrived,
    load_sem, halo_send, halo_recv, z_send, z_recv, part_send, part_recv, ready,
    occ, q_floor, q_span, small_sem,
):
    f32, bf16 = jnp.float32, jnp.bfloat16
    v = lax.axis_index("view")
    gx = lax.axis_index("gx")
    gy = lax.axis_index("gy")
    n_gx, n_gy = lax.axis_size("gx"), lax.axis_size("gy")

    def view(step):
        return lax.rem(v + VIEW + step, VIEW)

    x_next, x_prev = lax.rem(gx + 1, n_gx), lax.rem(gx + n_gx - 1, n_gx)
    y_next, y_prev = lax.rem(gy + 1, n_gy), lax.rem(gy + n_gy - 1, n_gy)

    barrier = pltpu.get_barrier_semaphore()
    for target in (
        {"gx": x_next}, {"gx": x_prev}, {"gy": y_next}, {"gy": y_prev},
        {"view": view(1)}, {"view": view(-1)},
    ):
        pl.semaphore_signal(barrier, inc=1, device_id=target, device_id_type=MESH)

    loads = []
    for j in range(CHUNKS):
        for c in range(3):
            load = pltpu.make_async_copy(
                vel.at[c, :, pl.ds(CUT * j, CUT)],
                cells.at[c, pl.ds(2, 32), pl.ds(8 + CUT * j, CUT)],
                load_sem.at[j, c],
            )
            load.start()
            loads.append(load)

    small = []
    for n, (src, dst) in enumerate(((occ_in, occ), (q_floor_in, q_floor), (q_span_in, q_span))):
        copy = pltpu.make_async_copy(src, dst, small_sem.at[n])
        copy.start()
        small.append(copy)

    row_id = lax.broadcasted_iota(jnp.int32, (256, 256), 0)
    col_id = lax.broadcasted_iota(jnp.int32, (256, 256), 1)
    depth_of = col_id % LANES
    chosen = ((row_id < LANES) & (depth_of < row_id)) | (depth_of == row_id - LANES)
    lower[...] = chosen.astype(f32).astype(bf16)

    to = lax.broadcasted_iota(jnp.int32, (LANES, LANES), 1)
    row = lax.broadcasted_iota(jnp.int32, (LANES, LANES), 0)

    def weight(gap):
        near = (gap == 1).astype(f32) - (gap == -1).astype(f32)
        far = (gap == 2).astype(f32) - (gap == -2).astype(f32)
        return (near - 0.125 * far).astype(bf16)

    own_weight = weight(row - to)
    halo_at = jnp.where(row % 4 < 2, row % 4 - 2, row % 4 + LANES - 2)
    halo_weight = weight(halo_at - to)
    for c in range(3):
        for n in range(3):
            stencils[c, pl.ds(LANES * n, LANES)] = own_weight
        stencils[c, pl.ds(3 * LANES, LANES)] = jnp.where(
            row // 8 == c, halo_weight, jnp.zeros_like(halo_weight)
        )

    lane = lax.broadcasted_iota(jnp.int32, (16, LANES), 1)
    pair_of = (lane % 8) // 2

    def pack(j):
        @pl.loop(0, CUT // 16)
        def _(t):
            rows = pl.ds(pl.multiple_of(8 + CUT * j + 16 * t, 8), 16)
            own = pl.ds(pl.multiple_of(CUT * j + 16 * t, 16), 16)
            for g in range(2):
                gathered = [jnp.zeros((16, LANES), f32) for s in range(4)]
                for k in range(4):
                    for c in range(3):
                        here = lane // 8 == 4 * k + c
                        for s in range(4):
                            u = cells[c, 2 + 16 * g + 4 * s + k, rows]
                            moved = pltpu.roll(u, (32 * k + 8 * c + 4) % LANES, 1)
                            gathered[s] = jnp.where(here, moved, gathered[s])
                left = right = None
                for s in range(4):
                    turned = gathered[s] if s == 2 else pltpu.roll(gathered[s], (2 * s - 4) % LANES, 1)
                    left = turned if s == 0 else jnp.where(pair_of == s, turned, left)
                    right = turned if s == 0 else jnp.where(pair_of == (s + 3) % 4, turned, right)
                send_l[g, own] = left
                send_r[g, own] = right

    halos = []

    def send_halo(number, src, dst, target):
        copy = pltpu.make_async_remote_copy(
            src_ref=src, dst_ref=dst, send_sem=halo_send.at[number], recv_sem=halo_recv.at[number],
            device_id=target, device_id_type=MESH,
        )
        copy.start()
        halos.append(copy)

    def enter():
        pl.semaphore_wait(barrier, 6)


        for n in range(2):
            half = pl.ds(64 * n, 64)
            send_halo(
                n, vel.at[:, pl.ds(30, 2), half],
                cells.at[:, pl.ds(0, 2), pl.ds(8 + 64 * n, 64)], {"gx": x_next},
            )
        send_halo(
            2, vel.at[:, :, pl.ds(0, 2)], cells.at[:, pl.ds(2, 32), pl.ds(136, 2)], {"gy": y_prev}
        )
        send_halo(
            3, vel.at[:, :, pl.ds(126, 2)], cells.at[:, pl.ds(2, 32), pl.ds(6, 2)], {"gy": y_next}
        )

    enter()

    z_copies = []
    for j in range(CHUNKS):
        for c in range(3):
            loads[3 * j + c].wait()
        pack(j)
        part = pl.ds(CUT * j, CUT)
        for side, (src, dst, step) in enumerate(((send_l, recv_l, -1), (send_r, recv_r, 1))):
            copy = pltpu.make_async_remote_copy(
                src_ref=src.at[:, part], dst_ref=dst.at[:, part], send_sem=z_send.at[j, side],
                recv_sem=z_recv.at[j, side], device_id={"view": view(step)}, device_id_type=MESH,
            )
            copy.start()
            z_copies.append(copy)

    @pl.loop(0, 32)
    def _(x):
        for c in range(3):
            for t in range(8):
                own = pl.ds(16 * t, 16)
                u = cells[c, 2 + x, pl.ds(8 + 16 * t, 16)]
                high = u.astype(bf16)
                rest = u - high.astype(f32)
                mid = rest.astype(bf16)
                low = (rest - mid.astype(f32)).astype(bf16)
                pieces[c, x, own, pl.ds(0, LANES)] = high
                pieces[c, x, own, pl.ds(LANES, LANES)] = mid
                pieces[c, x, own, pl.ds(2 * LANES, LANES)] = low

    send_halo(
        4, vel.at[:, pl.ds(0, 2)], cells.at[:, pl.ds(34, 2), pl.ds(8, 128)], {"gx": x_prev}
    )

    for j in range(CHUNKS):
        for copy in z_copies[2 * j : 2 * j + 2]:
            copy.wait_recv()
        if j == 0:
            for step in (2, -2):
                pl.semaphore_signal(
                    ready, inc=1, device_id={"view": view(step)}, device_id_type=MESH
                )

        @pl.loop(0, CUT // 8)
        def _(q):
            g, t = q % 2, q // 2
            own = pl.ds(pl.multiple_of(CUT * j + 16 * t, 16), 16)
            after, before = recv_l[g, own], recv_r[g, own]
            for s in range(4):
                both = jnp.where(pair_of == s, after, before)
                high = both.astype(bf16).astype(f32)
                rest = pltpu.roll(both - high, 4, 1)
                used = (pair_of == s) | (pair_of == (s + 3) % 4)
                halo = jnp.where(used, high, rest)
                for k in range(4):
                    placed = pltpu.roll(halo, (2 - 32 * k - 2 * s) % LANES, 1).astype(bf16)
                    for c in range(3):
                        pieces[c, 16 * g + 4 * s + k, own, pl.ds(3 * LANES, LANES)] = placed

    for copy in halos[2:4]:
        copy.wait_recv()

    for copy in small:
        copy.wait()

    unit = -(5.0 / (LANES * VIEW)) * math.log2(math.e)
    slope = -unit / (4.5 * q_span[0, 0])
    shift = -unit * q_floor[0, 0] / q_span[0, 0]

    def level_of(p, odd, k, t):
        x = 2 * p + k + 2
        top = 8 + 16 * t
        grad = []
        for c in range(3):
            def at(dx, dy):
                return cells[c, x + dx, pl.ds(top + dy, 16)]

            across = stencil(at(-2, 0), at(-1, 0), at(1, 0), at(2, 0))
            down = stencil(at(0, -2), at(0, -1), at(0, 1), at(0, 2))
            deep = deep_ref[odd, c, pl.ds(128 * k + 16 * t, 16)]
            grad.append((across, down, deep))
        squares = grad[0][0] * grad[0][0] + grad[1][1] * grad[1][1] + grad[2][2] * grad[2][2]
        cross = grad[0][1] * grad[1][0] + grad[0][2] * grad[2][0] + grad[1][2] * grad[2][1]
        total = (squares + cross) + cross
        factors = []
        for half in range(2):
            keep = occ[p // 4, 0, 2 * t + half].astype(f32)
            factors.append((slope * keep, shift * keep))
        m = jnp.concatenate([jnp.full((8, LANES), f[0], f32) for f in factors], axis=0)
        s = jnp.concatenate([jnp.full((8, LANES), f[1], f32) for f in factors], axis=0)
        return jnp.maximum(jnp.minimum(total * m + s, 0.0), unit)

    def turn_depth(p, odd):
        for c in range(3):
            deep_ref[odd, c] = jnp.dot(
                pieces[c, pl.ds(2 * p, 2)].reshape(256, 4 * LANES), stencils[c],
                preferred_element_type=f32,
            )

    def levels(p, odd, tiles=range(8)):
        for k in range(2):
            for t in tiles:
                lev = level_of(p, odd, k, t)
                high = lev.astype(bf16)
                low = (lev - high.astype(f32)).astype(bf16)
                here = pl.ds(128 * k + 16 * t, 16)
                split[odd, here, pl.ds(0, LANES)] = high
                split[odd, here, pl.ds(LANES, LANES)] = low

    def finish(p, odd):
        turned = lax.dot_general(
            lower[...], split[odd], (((1,), (1,)), ((), ())), preferred_element_type=f32
        )
        first = jnp.zeros((8, 256), f32)
        second = jnp.zeros((8, 256), f32)
        for z in range(16):
            passing = jnp.exp2(turned[8 * z : 8 * z + 8])
            lev = turned[128 + 8 * z : 136 + 8 * z]
            left = passing * jnp.exp2(lev)
            one = (passing - left) * lev
            first = first + one
            second = second + one * lev
        rows = [
            jnp.sum(first, axis=0, keepdims=True),
            jnp.sum(second, axis=0, keepdims=True),
            left[7:8],
        ]
        for q in range(3):
            for k in range(2):
                parts[p // 2, pl.ds(4 * q + 2 * (p % 2) + k, 1)] = rows[q][:, 128 * k : 128 * k + 128]

    def part_copy(b, source):
        return pltpu.make_async_remote_copy(
            src_ref=parts.at[b], dst_ref=arrived.at[source], send_sem=part_send.at[b],
            recv_sem=part_recv.at[source], device_id={"view": b}, device_id_type=MESH,
        )

    def hand_over(b):
        @pl.when(b != v)
        def _():
            part_copy(b, v).start()

        @pl.when(b == v)
        def _():
            arrived[v] = parts[b]

    def two_pairs(p):
        turn_depth(p, 0)
        finish(p - 1, 1)
        levels(p, 0)
        turn_depth(p + 1, 1)
        finish(p, 0)
        levels(p + 1, 1)

    turn_depth(1, 1)
    levels(1, 1)

    @pl.loop(1, 4)
    def _(b):
        two_pairs(2 * b)

        @pl.when(b == 2)
        def _():
            pl.semaphore_wait(ready, 2)

        @pl.when(b > 1)
        def _():
            hand_over(b - 1)

    turn_depth(0, 0)
    finish(7, 1)
    hand_over(3)

    for n in range(2):
        halos[n].wait_recv()
        levels(0, 0, range(4 * n, 4 * n + 4))
    finish(0, 0)
    hand_over(0)

    turn_depth(8, 1)
    levels(8, 1)

    @pl.loop(4, 7)
    def _(b):
        two_pairs(2 * b + 1)
        hand_over(b)

    turn_depth(15, 0)
    finish(14, 1)
    halos[4].wait_recv()
    levels(15, 0)
    finish(15, 0)
    hand_over(7)

    for step in range(1, VIEW):
        part_copy(view(step), view(step)).wait_recv()

    red = jnp.zeros((ROWS, LANES), f32)
    green = jnp.zeros((ROWS, LANES), f32)
    ahead = jnp.ones((ROWS, LANES), f32)
    for s in range(VIEW):
        red = red + ahead * arrived[s, 0:4]
        green = green + ahead * arrived[s, 4:8]
        ahead = ahead * arrived[s, 8:12]
    red = red * (1.0 / unit)
    green = 4.0 * (red - green * (1.0 / (unit * unit)))
    out[0, 0, 0] = red
    out[0, 0, 1] = green
    out[0, 0, 2] = (1.0 - ahead) - red
    out[0, 0, 3] = 1.0 - ahead

    for copy in halos + z_copies:
        copy.wait_send()
    for step in range(1, VIEW):
        part_copy(view(step), v).wait_send()


def local(velocity, occupied, q_floor, q_span):
    f32, bf16 = jnp.float32, jnp.bfloat16
    here = pl.BlockSpec(memory_space=pltpu.HBM)
    return pl.pallas_call(
        kernel,
        out_shape=jax.ShapeDtypeStruct((1, 1, 4, ROWS, LANES), f32),
        in_specs=[here] * 4,
        out_specs=pl.BlockSpec(memory_space=pltpu.VMEM),
        scratch_shapes=[
            pltpu.VMEM((3, 36, 144, LANES), f32),
            pltpu.VMEM((3, 32, 128, 4 * LANES), bf16),
            pltpu.VMEM((3, 4 * LANES, LANES), bf16),
            pltpu.VMEM((2, 128, LANES), f32),
            pltpu.VMEM((2, 128, LANES), f32),
            pltpu.VMEM((2, 128, LANES), f32),
            pltpu.VMEM((2, 128, LANES), f32),
            pltpu.VMEM((2, 3, 256, LANES), f32),
            pltpu.VMEM((2, 256, 256), bf16),
            pltpu.VMEM((256, 256), bf16),
            pltpu.VMEM((VIEW, 16, LANES), f32),
            pltpu.VMEM((VIEW, 16, LANES), f32),
            pltpu.SemaphoreType.DMA((CHUNKS, 3)),
            pltpu.SemaphoreType.DMA((5,)),
            pltpu.SemaphoreType.DMA((5,)),
            pltpu.SemaphoreType.DMA((CHUNKS, 2)),
            pltpu.SemaphoreType.DMA((CHUNKS, 2)),
            pltpu.SemaphoreType.DMA((VIEW,)),
            pltpu.SemaphoreType.DMA((VIEW,)),
            pltpu.SemaphoreType.REGULAR,
            pltpu.SMEM((4, 1, 16), jnp.int32),
            pltpu.SMEM((1, 1), f32),
            pltpu.SMEM((1, 1), f32),
            pltpu.SemaphoreType.DMA((3,)),
        ],
        compiler_params=pltpu.CompilerParams(collective_id=0, has_side_effects=True),
    )(velocity, occupied.transpose(0, 2, 1), q_floor.reshape(1, 1), q_span.reshape(1, 1))


def solution(mesh):
    placed = (P(None, "gx", "gy", "view"), P("gx", "gy", "view"), P(), P())
    return jax.shard_map(
        local,
        mesh=mesh,
        in_specs=placed,
        out_specs=P("gx", "gy", None, "view", None),
        check_vma=False,
    )
```

```python
import functools
import math

import jax
import jax.numpy as jnp
from jax import lax
from jax.experimental import pallas as pl
from jax.experimental.pallas import tpu as pltpu
from jax.sharding import PartitionSpec as P

MESH = pl.DeviceIdType.MESH
SUB = 8
LANES = 128
ROWS = 4
VIEW = 8
CHUNKS = 4
CUT = 128 // CHUNKS


def stencil(a, b, c, d):
    return (c - b) - 0.125 * (d - a)


def kernel(
    vel, occ_in, q_floor, q_span, out,
    cells, pieces, stencils, send_l, send_r, recv_l, recv_r, deep_ref, split, lower, parts, arrived,
    load_sem, halo_send, halo_recv, z_send, z_recv, part_send, part_recv, ready,
    occ, small_sem,
):
    f32, bf16 = jnp.float32, jnp.bfloat16
    v = lax.axis_index("view")
    gx = lax.axis_index("gx")
    gy = lax.axis_index("gy")
    n_gx, n_gy = lax.axis_size("gx"), lax.axis_size("gy")

    def view(step):
        return lax.rem(v + VIEW + step, VIEW)

    x_next, x_prev = lax.rem(gx + 1, n_gx), lax.rem(gx + n_gx - 1, n_gx)
    y_next, y_prev = lax.rem(gy + 1, n_gy), lax.rem(gy + n_gy - 1, n_gy)

    barrier = pltpu.get_barrier_semaphore()
    for target in (
        {"gx": x_next}, {"gx": x_prev}, {"gy": y_next}, {"gy": y_prev},
        {"view": view(1)}, {"view": view(-1)},
    ):
        pl.semaphore_signal(barrier, inc=1, device_id=target, device_id_type=MESH)

    loads = []
    for j in range(CHUNKS):
        for c in range(3):
            load = pltpu.make_async_copy(
                vel.at[c, :, pl.ds(CUT * j, CUT)],
                cells.at[c, pl.ds(2, 32), pl.ds(8 + CUT * j, CUT)],
                load_sem.at[j, c],
            )
            load.start()
            loads.append(load)

    small = []
    for n, (src, dst) in enumerate(((occ_in, occ),)):
        copy = pltpu.make_async_copy(src, dst, small_sem.at[n])
        copy.start()
        small.append(copy)

    row_id = lax.broadcasted_iota(jnp.int32, (256, 256), 0)
    col_id = lax.broadcasted_iota(jnp.int32, (256, 256), 1)
    depth_of = col_id % LANES
    chosen = ((row_id < LANES) & (depth_of < row_id)) | (depth_of == row_id - LANES)
    lower[...] = chosen.astype(f32).astype(bf16)

    to = lax.broadcasted_iota(jnp.int32, (LANES, LANES), 1)
    row = lax.broadcasted_iota(jnp.int32, (LANES, LANES), 0)

    def weight(gap):
        near = (gap == 1).astype(f32) - (gap == -1).astype(f32)
        far = (gap == 2).astype(f32) - (gap == -2).astype(f32)
        return (near - 0.125 * far).astype(bf16)

    own_weight = weight(row - to)
    halo_at = jnp.where(row % 4 < 2, row % 4 - 2, row % 4 + LANES - 2)
    halo_weight = weight(halo_at - to)
    for c in range(3):
        for n in range(3):
            stencils[c, pl.ds(LANES * n, LANES)] = own_weight
        stencils[c, pl.ds(3 * LANES, LANES)] = jnp.where(
            row // 8 == c, halo_weight, jnp.zeros_like(halo_weight)
        )

    lane = lax.broadcasted_iota(jnp.int32, (16, LANES), 1)
    pair_of = (lane % 8) // 2

    def pack(j):
        @pl.loop(0, CUT // 16)
        def _(t):
            rows = pl.ds(pl.multiple_of(8 + CUT * j + 16 * t, 8), 16)
            own = pl.ds(pl.multiple_of(CUT * j + 16 * t, 16), 16)
            for g in range(2):
                gathered = [jnp.zeros((16, LANES), f32) for s in range(4)]
                for k in range(4):
                    for c in range(3):
                        here = lane // 8 == 4 * k + c
                        for s in range(4):
                            u = cells[c, 2 + 16 * g + 4 * s + k, rows]
                            moved = pltpu.roll(u, (32 * k + 8 * c + 4) % LANES, 1)
                            gathered[s] = jnp.where(here, moved, gathered[s])
                left = right = None
                for s in range(4):
                    turned = gathered[s] if s == 2 else pltpu.roll(gathered[s], (2 * s - 4) % LANES, 1)
                    left = turned if s == 0 else jnp.where(pair_of == s, turned, left)
                    right = turned if s == 0 else jnp.where(pair_of == (s + 3) % 4, turned, right)
                send_l[g, own] = left
                send_r[g, own] = right

    halos = []

    def send_halo(number, src, dst, target):
        copy = pltpu.make_async_remote_copy(
            src_ref=src, dst_ref=dst, send_sem=halo_send.at[number], recv_sem=halo_recv.at[number],
            device_id=target, device_id_type=MESH,
        )
        copy.start()
        halos.append(copy)

    def enter():
        pl.semaphore_wait(barrier, 6)


        for n in range(2):
            half = pl.ds(64 * n, 64)
            send_halo(
                n, vel.at[:, pl.ds(30, 2), half],
                cells.at[:, pl.ds(0, 2), pl.ds(8 + 64 * n, 64)], {"gx": x_next},
            )
        send_halo(
            2, vel.at[:, :, pl.ds(0, 2)], cells.at[:, pl.ds(2, 32), pl.ds(136, 2)], {"gy": y_prev}
        )
        send_halo(
            3, vel.at[:, :, pl.ds(126, 2)], cells.at[:, pl.ds(2, 32), pl.ds(6, 2)], {"gy": y_next}
        )

    enter()

    z_copies = []
    for j in range(CHUNKS):
        for c in range(3):
            loads[3 * j + c].wait()
        pack(j)
        part = pl.ds(CUT * j, CUT)
        for side, (src, dst, step) in enumerate(((send_l, recv_l, -1), (send_r, recv_r, 1))):
            copy = pltpu.make_async_remote_copy(
                src_ref=src.at[:, part], dst_ref=dst.at[:, part], send_sem=z_send.at[j, side],
                recv_sem=z_recv.at[j, side], device_id={"view": view(step)}, device_id_type=MESH,
            )
            copy.start()
            z_copies.append(copy)

    @pl.loop(0, 32)
    def _(x):
        for c in range(3):
            for t in range(8):
                own = pl.ds(16 * t, 16)
                u = cells[c, 2 + x, pl.ds(8 + 16 * t, 16)]
                high = u.astype(bf16)
                rest = u - high.astype(f32)
                mid = rest.astype(bf16)
                low = (rest - mid.astype(f32)).astype(bf16)
                pieces[c, x, own, pl.ds(0, LANES)] = high
                pieces[c, x, own, pl.ds(LANES, LANES)] = mid
                pieces[c, x, own, pl.ds(2 * LANES, LANES)] = low

    send_halo(
        4, vel.at[:, pl.ds(0, 2)], cells.at[:, pl.ds(34, 2), pl.ds(8, 128)], {"gx": x_prev}
    )

    for j in range(CHUNKS):
        for copy in z_copies[2 * j : 2 * j + 2]:
            copy.wait_recv()
        if j == 0:
            for step in (2, -2):
                pl.semaphore_signal(
                    ready, inc=1, device_id={"view": view(step)}, device_id_type=MESH
                )

        @pl.loop(0, CUT // 8)
        def _(q):
            g, t = q % 2, q // 2
            own = pl.ds(pl.multiple_of(CUT * j + 16 * t, 16), 16)
            after, before = recv_l[g, own], recv_r[g, own]
            for s in range(4):
                both = jnp.where(pair_of == s, after, before)
                high = both.astype(bf16).astype(f32)
                rest = pltpu.roll(both - high, 4, 1)
                used = (pair_of == s) | (pair_of == (s + 3) % 4)
                halo = jnp.where(used, high, rest)
                for k in range(4):
                    placed = pltpu.roll(halo, (2 - 32 * k - 2 * s) % LANES, 1).astype(bf16)
                    for c in range(3):
                        pieces[c, 16 * g + 4 * s + k, own, pl.ds(3 * LANES, LANES)] = placed

    for copy in halos[2:4]:
        copy.wait_recv()

    for copy in small:
        copy.wait()

    unit = -(5.0 / (LANES * VIEW)) * math.log2(math.e)
    slope = -unit / (4.5 * q_span[0])
    shift = -unit * q_floor[0] / q_span[0]

    def level_of(p, odd, k, t):
        x = 2 * p + k + 2
        top = 8 + 16 * t
        grad = []
        for c in range(3):
            def at(dx, dy):
                return cells[c, x + dx, pl.ds(top + dy, 16)]

            across = stencil(at(-2, 0), at(-1, 0), at(1, 0), at(2, 0))
            down = stencil(at(0, -2), at(0, -1), at(0, 1), at(0, 2))
            deep = deep_ref[odd, c, pl.ds(128 * k + 16 * t, 16)]
            grad.append((across, down, deep))
        squares = grad[0][0] * grad[0][0] + grad[1][1] * grad[1][1] + grad[2][2] * grad[2][2]
        cross = grad[0][1] * grad[1][0] + grad[0][2] * grad[2][0] + grad[1][2] * grad[2][1]
        total = (squares + cross) + cross
        factors = []
        for half in range(2):
            keep = occ[p // 4, 0, 2 * t + half].astype(f32)
            factors.append((slope * keep, shift * keep))
        m = jnp.concatenate([jnp.full((8, LANES), f[0], f32) for f in factors], axis=0)
        s = jnp.concatenate([jnp.full((8, LANES), f[1], f32) for f in factors], axis=0)
        return jnp.maximum(jnp.minimum(total * m + s, 0.0), unit)

    def turn_depth(p, odd):
        for c in range(3):
            deep_ref[odd, c] = jnp.dot(
                pieces[c, pl.ds(2 * p, 2)].reshape(256, 4 * LANES), stencils[c],
                preferred_element_type=f32,
            )

    def levels(p, odd, tiles=range(8)):
        for k in range(2):
            for t in tiles:
                lev = level_of(p, odd, k, t)
                high = lev.astype(bf16)
                low = (lev - high.astype(f32)).astype(bf16)
                here = pl.ds(128 * k + 16 * t, 16)
                split[odd, here, pl.ds(0, LANES)] = high
                split[odd, here, pl.ds(LANES, LANES)] = low

    def finish(p, odd):
        turned = lax.dot_general(
            lower[...], split[odd], (((1,), (1,)), ((), ())), preferred_element_type=f32
        )
        first = jnp.zeros((8, 256), f32)
        second = jnp.zeros((8, 256), f32)
        for z in range(16):
            passing = jnp.exp2(turned[8 * z : 8 * z + 8])
            lev = turned[128 + 8 * z : 136 + 8 * z]
            left = passing * jnp.exp2(lev)
            one = (passing - left) * lev
            first = first + one
            second = second + one * lev
        rows = [
            jnp.sum(first, axis=0, keepdims=True),
            jnp.sum(second, axis=0, keepdims=True),
            left[7:8],
        ]
        for q in range(3):
            for k in range(2):
                parts[p // 2, pl.ds(4 * q + 2 * (p % 2) + k, 1)] = rows[q][:, 128 * k : 128 * k + 128]

    def part_copy(b, source):
        return pltpu.make_async_remote_copy(
            src_ref=parts.at[b], dst_ref=arrived.at[source], send_sem=part_send.at[b],
            recv_sem=part_recv.at[source], device_id={"view": b}, device_id_type=MESH,
        )

    def hand_over(b):
        @pl.when(b != v)
        def _():
            part_copy(b, v).start()

        @pl.when(b == v)
        def _():
            arrived[v] = parts[b]

    def two_pairs(p):
        turn_depth(p, 0)
        finish(p - 1, 1)
        levels(p, 0)
        turn_depth(p + 1, 1)
        finish(p, 0)
        levels(p + 1, 1)

    turn_depth(1, 1)
    levels(1, 1)

    @pl.loop(1, 4)
    def _(b):
        two_pairs(2 * b)

        @pl.when(b == 2)
        def _():
            pl.semaphore_wait(ready, 2)

        @pl.when(b > 1)
        def _():
            hand_over(b - 1)

    turn_depth(0, 0)
    finish(7, 1)
    hand_over(3)

    for n in range(2):
        halos[n].wait_recv()
        levels(0, 0, range(4 * n, 4 * n + 4))
    finish(0, 0)
    hand_over(0)

    turn_depth(8, 1)
    levels(8, 1)

    @pl.loop(4, 7)
    def _(b):
        two_pairs(2 * b + 1)
        hand_over(b)

    turn_depth(15, 0)
    finish(14, 1)
    halos[4].wait_recv()
    levels(15, 0)
    finish(15, 0)
    hand_over(7)

    for step in range(1, VIEW):
        part_copy(view(step), view(step)).wait_recv()

    red = jnp.zeros((ROWS, LANES), f32)
    green = jnp.zeros((ROWS, LANES), f32)
    ahead = jnp.ones((ROWS, LANES), f32)
    for s in range(VIEW):
        red = red + ahead * arrived[s, 0:4]
        green = green + ahead * arrived[s, 4:8]
        ahead = ahead * arrived[s, 8:12]
    red = red * (1.0 / unit)
    green = 4.0 * (red - green * (1.0 / (unit * unit)))
    out[0, 0, 0] = red
    out[0, 0, 1] = green
    out[0, 0, 2] = (1.0 - ahead) - red
    out[0, 0, 3] = 1.0 - ahead

    for copy in halos + z_copies:
        copy.wait_send()
    for step in range(1, VIEW):
        part_copy(view(step), v).wait_send()


def local(velocity, occupied, q_floor, q_span):
    f32, bf16 = jnp.float32, jnp.bfloat16
    here = pl.BlockSpec(memory_space=pltpu.HBM)
    return pl.pallas_call(
        kernel,
        out_shape=pltpu.VMEM((1, 1, 4, ROWS, LANES), f32),
        in_specs=[here, here] + [pl.BlockSpec(memory_space=pltpu.SMEM)] * 2,
        out_specs=pl.BlockSpec(memory_space=pltpu.VMEM),
        scratch_shapes=[
            pltpu.VMEM((3, 36, 144, LANES), f32),
            pltpu.VMEM((3, 32, 128, 4 * LANES), bf16),
            pltpu.VMEM((3, 4 * LANES, LANES), bf16),
            pltpu.VMEM((2, 128, LANES), f32),
            pltpu.VMEM((2, 128, LANES), f32),
            pltpu.VMEM((2, 128, LANES), f32),
            pltpu.VMEM((2, 128, LANES), f32),
            pltpu.VMEM((2, 3, 256, LANES), f32),
            pltpu.VMEM((2, 256, 256), bf16),
            pltpu.VMEM((256, 256), bf16),
            pltpu.VMEM((VIEW, 16, LANES), f32),
            pltpu.VMEM((VIEW, 16, LANES), f32),
            pltpu.SemaphoreType.DMA((CHUNKS, 3)),
            pltpu.SemaphoreType.DMA((5,)),
            pltpu.SemaphoreType.DMA((5,)),
            pltpu.SemaphoreType.DMA((CHUNKS, 2)),
            pltpu.SemaphoreType.DMA((CHUNKS, 2)),
            pltpu.SemaphoreType.DMA((VIEW,)),
            pltpu.SemaphoreType.DMA((VIEW,)),
            pltpu.SemaphoreType.REGULAR,
            pltpu.SMEM((4, 1, 16), jnp.int32),
            pltpu.SemaphoreType.DMA((3,)),
        ],
        compiler_params=pltpu.CompilerParams(collective_id=0, has_side_effects=True),
    )(velocity, occupied.transpose(0, 2, 1), q_floor, q_span)


def solution(mesh):
    placed = (P(None, "gx", "gy", "view"), P("gx", "gy", "view"), P(), P())
    return jax.shard_map(
        local,
        mesh=mesh,
        in_specs=placed,
        out_specs=P("gx", "gy", None, "view", None),
        check_vma=False,
    )
```

```python
import functools
import math

import jax
import jax.numpy as jnp
from jax import lax
from jax.experimental import pallas as pl
from jax.experimental.pallas import tpu as pltpu
from jax.sharding import PartitionSpec as P

MESH = pl.DeviceIdType.MESH
SUB = 8
LANES = 128
ROWS = 4
VIEW = 8
CHUNKS = 4
CUT = 128 // CHUNKS


def stencil(a, b, c, d):
    return (c - b) - 0.125 * (d - a)


def kernel(
    vel, occ_in, q_floor, q_span, out,
    cells, pieces, stencils, send_l, send_r, recv_l, recv_r, deep_ref, split, lower, parts, arrived,
    load_sem, halo_send, halo_recv, z_send, z_recv, part_send, part_recv, ready,
    occ, small_sem,
):
    f32, bf16 = jnp.float32, jnp.bfloat16
    v = lax.axis_index("view")
    gx = lax.axis_index("gx")
    gy = lax.axis_index("gy")
    n_gx, n_gy = lax.axis_size("gx"), lax.axis_size("gy")

    def view(step):
        return lax.rem(v + VIEW + step, VIEW)

    x_next, x_prev = lax.rem(gx + 1, n_gx), lax.rem(gx + n_gx - 1, n_gx)
    y_next, y_prev = lax.rem(gy + 1, n_gy), lax.rem(gy + n_gy - 1, n_gy)

    barrier = pltpu.get_barrier_semaphore()
    for target in (
        {"gx": x_next}, {"gx": x_prev}, {"gy": y_next}, {"gy": y_prev},
        {"view": view(1)}, {"view": view(-1)},
    ):
        pl.semaphore_signal(barrier, inc=1, device_id=target, device_id_type=MESH)

    loads = []
    for j in range(CHUNKS):
        for c in range(3):
            load = pltpu.make_async_copy(
                vel.at[c, :, pl.ds(CUT * j, CUT)],
                cells.at[c, pl.ds(2, 32), pl.ds(8 + CUT * j, CUT)],
                load_sem.at[j, c],
            )
            load.start()
            loads.append(load)

    small = []
    for n, (src, dst) in enumerate(((occ_in, occ),)):
        copy = pltpu.make_async_copy(src, dst, small_sem.at[n])
        copy.start()
        small.append(copy)

    row_id = lax.broadcasted_iota(jnp.int32, (256, 256), 0)
    col_id = lax.broadcasted_iota(jnp.int32, (256, 256), 1)
    depth_of = col_id % LANES
    chosen = ((row_id < LANES) & (depth_of < row_id)) | (depth_of == row_id - LANES)
    lower[...] = chosen.astype(f32).astype(bf16)

    to = lax.broadcasted_iota(jnp.int32, (LANES, LANES), 1)
    row = lax.broadcasted_iota(jnp.int32, (LANES, LANES), 0)

    def weight(gap):
        near = (gap == 1).astype(f32) - (gap == -1).astype(f32)
        far = (gap == 2).astype(f32) - (gap == -2).astype(f32)
        return (near - 0.125 * far).astype(bf16)

    own_weight = weight(row - to)
    halo_at = jnp.where(row % 4 < 2, row % 4 - 2, row % 4 + LANES - 2)
    halo_weight = weight(halo_at - to)
    for c in range(3):
        for n in range(3):
            stencils[c, pl.ds(LANES * n, LANES)] = own_weight
        stencils[c, pl.ds(3 * LANES, LANES)] = jnp.where(
            row // 8 == c, halo_weight, jnp.zeros_like(halo_weight)
        )

    lane = lax.broadcasted_iota(jnp.int32, (16, LANES), 1)
    pair_of = (lane % 8) // 2

    def pack(j):
        @pl.loop(0, CUT // 16)
        def _(t):
            rows = pl.ds(pl.multiple_of(8 + CUT * j + 16 * t, 8), 16)
            own = pl.ds(pl.multiple_of(CUT * j + 16 * t, 16), 16)
            for g in range(2):
                gathered = [jnp.zeros((16, LANES), f32) for s in range(4)]
                for k in range(4):
                    for c in range(3):
                        here = lane // 8 == 4 * k + c
                        for s in range(4):
                            u = cells[c, 2 + 16 * g + 4 * s + k, rows]
                            moved = pltpu.roll(u, (32 * k + 8 * c + 4) % LANES, 1)
                            gathered[s] = jnp.where(here, moved, gathered[s])
                left = right = None
                for s in range(4):
                    turned = gathered[s] if s == 2 else pltpu.roll(gathered[s], (2 * s - 4) % LANES, 1)
                    left = turned if s == 0 else jnp.where(pair_of == s, turned, left)
                    right = turned if s == 0 else jnp.where(pair_of == (s + 3) % 4, turned, right)
                send_l[g, own] = left
                send_r[g, own] = right

    halos = []

    def send_halo(number, src, dst, target):
        copy = pltpu.make_async_remote_copy(
            src_ref=src, dst_ref=dst, send_sem=halo_send.at[number], recv_sem=halo_recv.at[number],
            device_id=target, device_id_type=MESH,
        )
        copy.start()
        halos.append(copy)

    def enter():
        pl.semaphore_wait(barrier, 6)


        for n in range(2):
            half = pl.ds(64 * n, 64)
            send_halo(
                n, vel.at[:, pl.ds(30, 2), half],
                cells.at[:, pl.ds(0, 2), pl.ds(8 + 64 * n, 64)], {"gx": x_next},
            )
        send_halo(
            2, vel.at[:, :, pl.ds(0, 2)], cells.at[:, pl.ds(2, 32), pl.ds(136, 2)], {"gy": y_prev}
        )
        send_halo(
            3, vel.at[:, :, pl.ds(126, 2)], cells.at[:, pl.ds(2, 32), pl.ds(6, 2)], {"gy": y_next}
        )

    enter()

    z_copies = []
    for j in range(CHUNKS):
        for c in range(3):
            loads[3 * j + c].wait()
        pack(j)
        part = pl.ds(CUT * j, CUT)
        for side, (src, dst, step) in enumerate(((send_l, recv_l, -1), (send_r, recv_r, 1))):
            copy = pltpu.make_async_remote_copy(
                src_ref=src.at[:, part], dst_ref=dst.at[:, part], send_sem=z_send.at[j, side],
                recv_sem=z_recv.at[j, side], device_id={"view": view(step)}, device_id_type=MESH,
            )
            copy.start()
            z_copies.append(copy)

    send_halo(
        4, vel.at[:, pl.ds(0, 2)], cells.at[:, pl.ds(34, 2), pl.ds(8, 128)], {"gx": x_prev}
    )

    @pl.loop(0, 32)
    def _(x):
        for c in range(3):
            for t in range(8):
                own = pl.ds(16 * t, 16)
                u = cells[c, 2 + x, pl.ds(8 + 16 * t, 16)]
                high = u.astype(bf16)
                rest = u - high.astype(f32)
                mid = rest.astype(bf16)
                low = (rest - mid.astype(f32)).astype(bf16)
                pieces[c, x, own, pl.ds(0, LANES)] = high
                pieces[c, x, own, pl.ds(LANES, LANES)] = mid
                pieces[c, x, own, pl.ds(2 * LANES, LANES)] = low

    for j in range(CHUNKS):
        for copy in z_copies[2 * j : 2 * j + 2]:
            copy.wait_recv()
        if j == 0:
            for step in (2, -2):
                pl.semaphore_signal(
                    ready, inc=1, device_id={"view": view(step)}, device_id_type=MESH
                )

        @pl.loop(0, CUT // 8)
        def _(q):
            g, t = q % 2, q // 2
            own = pl.ds(pl.multiple_of(CUT * j + 16 * t, 16), 16)
            after, before = recv_l[g, own], recv_r[g, own]
            for s in range(4):
                both = jnp.where(pair_of == s, after, before)
                high = both.astype(bf16).astype(f32)
                rest = pltpu.roll(both - high, 4, 1)
                used = (pair_of == s) | (pair_of == (s + 3) % 4)
                halo = jnp.where(used, high, rest)
                for k in range(4):
                    placed = pltpu.roll(halo, (2 - 32 * k - 2 * s) % LANES, 1).astype(bf16)
                    for c in range(3):
                        pieces[c, 16 * g + 4 * s + k, own, pl.ds(3 * LANES, LANES)] = placed

    for copy in halos[2:4]:
        copy.wait_recv()

    for copy in small:
        copy.wait()

    unit = -(5.0 / (LANES * VIEW)) * math.log2(math.e)
    slope = -unit / (4.5 * q_span[0])
    shift = -unit * q_floor[0] / q_span[0]

    def level_of(p, odd, k, t):
        x = 2 * p + k + 2
        top = 8 + 16 * t
        grad = []
        for c in range(3):
            def at(dx, dy):
                return cells[c, x + dx, pl.ds(top + dy, 16)]

            across = stencil(at(-2, 0), at(-1, 0), at(1, 0), at(2, 0))
            down = stencil(at(0, -2), at(0, -1), at(0, 1), at(0, 2))
            deep = deep_ref[odd, c, pl.ds(128 * k + 16 * t, 16)]
            grad.append((across, down, deep))
        squares = grad[0][0] * grad[0][0] + grad[1][1] * grad[1][1] + grad[2][2] * grad[2][2]
        cross = grad[0][1] * grad[1][0] + grad[0][2] * grad[2][0] + grad[1][2] * grad[2][1]
        total = (squares + cross) + cross
        factors = []
        for half in range(2):
            keep = occ[p // 4, 0, 2 * t + half].astype(f32)
            factors.append((slope * keep, shift * keep))
        m = jnp.concatenate([jnp.full((8, LANES), f[0], f32) for f in factors], axis=0)
        s = jnp.concatenate([jnp.full((8, LANES), f[1], f32) for f in factors], axis=0)
        return jnp.maximum(jnp.minimum(total * m + s, 0.0), unit)

    def turn_depth(p, odd):
        for c in range(3):
            deep_ref[odd, c] = jnp.dot(
                pieces[c, pl.ds(2 * p, 2)].reshape(256, 4 * LANES), stencils[c],
                preferred_element_type=f32,
            )

    def levels(p, odd, tiles=range(8)):
        for k in range(2):
            for t in tiles:
                lev = level_of(p, odd, k, t)
                high = lev.astype(bf16)
                low = (lev - high.astype(f32)).astype(bf16)
                here = pl.ds(128 * k + 16 * t, 16)
                split[odd, here, pl.ds(0, LANES)] = high
                split[odd, here, pl.ds(LANES, LANES)] = low

    def finish(p, odd):
        turned = lax.dot_general(
            lower[...], split[odd], (((1,), (1,)), ((), ())), preferred_element_type=f32
        )
        first = jnp.zeros((8, 256), f32)
        second = jnp.zeros((8, 256), f32)
        for z in range(16):
            passing = jnp.exp2(turned[8 * z : 8 * z + 8])
            lev = turned[128 + 8 * z : 136 + 8 * z]
            left = passing * jnp.exp2(lev)
            one = (passing - left) * lev
            first = first + one
            second = second + one * lev
        rows = [
            jnp.sum(first, axis=0, keepdims=True),
            jnp.sum(second, axis=0, keepdims=True),
            left[7:8],
        ]
        for q in range(3):
            for k in range(2):
                parts[p // 2, pl.ds(4 * q + 2 * (p % 2) + k, 1)] = rows[q][:, 128 * k : 128 * k + 128]

    def part_copy(b, source):
        return pltpu.make_async_remote_copy(
            src_ref=parts.at[b], dst_ref=arrived.at[source], send_sem=part_send.at[b],
            recv_sem=part_recv.at[source], device_id={"view": b}, device_id_type=MESH,
        )

    def hand_over(b):
        @pl.when(b != v)
        def _():
            part_copy(b, v).start()

        @pl.when(b == v)
        def _():
            arrived[v] = parts[b]

    def two_pairs(p):
        turn_depth(p, 0)
        finish(p - 1, 1)
        levels(p, 0)
        turn_depth(p + 1, 1)
        finish(p, 0)
        levels(p + 1, 1)

    turn_depth(1, 1)
    levels(1, 1)

    @pl.loop(1, 4)
    def _(b):
        two_pairs(2 * b)

        @pl.when(b == 2)
        def _():
            pl.semaphore_wait(ready, 2)

        @pl.when(b > 1)
        def _():
            hand_over(b - 1)

    turn_depth(0, 0)
    finish(7, 1)
    hand_over(3)

    for n in range(2):
        halos[n].wait_recv()
        levels(0, 0, range(4 * n, 4 * n + 4))
    finish(0, 0)
    hand_over(0)

    turn_depth(8, 1)
    levels(8, 1)

    @pl.loop(4, 7)
    def _(b):
        two_pairs(2 * b + 1)
        hand_over(b)

    turn_depth(15, 0)
    finish(14, 1)
    halos[4].wait_recv()
    levels(15, 0)
    finish(15, 0)
    hand_over(7)

    for copy in halos + z_copies:
        copy.wait_send()
    for step in range(1, VIEW):
        part_copy(view(step), v).wait_send()
    for step in range(1, VIEW):
        part_copy(view(step), view(step)).wait_recv()

    red = jnp.zeros((ROWS, LANES), f32)
    green = jnp.zeros((ROWS, LANES), f32)
    ahead = jnp.ones((ROWS, LANES), f32)
    for s in range(VIEW):
        red = red + ahead * arrived[s, 0:4]
        green = green + ahead * arrived[s, 4:8]
        ahead = ahead * arrived[s, 8:12]
    red = red * (1.0 / unit)
    green = 4.0 * (red - green * (1.0 / (unit * unit)))
    out[0, 0, 0] = red
    out[0, 0, 1] = green
    out[0, 0, 2] = (1.0 - ahead) - red
    out[0, 0, 3] = 1.0 - ahead


def local(velocity, occupied, q_floor, q_span):
    f32, bf16 = jnp.float32, jnp.bfloat16
    here = pl.BlockSpec(memory_space=pltpu.HBM)
    return pl.pallas_call(
        kernel,
        out_shape=pltpu.VMEM((1, 1, 4, ROWS, LANES), f32),
        in_specs=[here, here] + [pl.BlockSpec(memory_space=pltpu.SMEM)] * 2,
        out_specs=pl.BlockSpec(memory_space=pltpu.VMEM),
        scratch_shapes=[
            pltpu.VMEM((3, 36, 144, LANES), f32),
            pltpu.VMEM((3, 32, 128, 4 * LANES), bf16),
            pltpu.VMEM((3, 4 * LANES, LANES), bf16),
            pltpu.VMEM((2, 128, LANES), f32),
            pltpu.VMEM((2, 128, LANES), f32),
            pltpu.VMEM((2, 128, LANES), f32),
            pltpu.VMEM((2, 128, LANES), f32),
            pltpu.VMEM((2, 3, 256, LANES), f32),
            pltpu.VMEM((2, 256, 256), bf16),
            pltpu.VMEM((256, 256), bf16),
            pltpu.VMEM((VIEW, 16, LANES), f32),
            pltpu.VMEM((VIEW, 16, LANES), f32),
            pltpu.SemaphoreType.DMA((CHUNKS, 3)),
            pltpu.SemaphoreType.DMA((5,)),
            pltpu.SemaphoreType.DMA((5,)),
            pltpu.SemaphoreType.DMA((CHUNKS, 2)),
            pltpu.SemaphoreType.DMA((CHUNKS, 2)),
            pltpu.SemaphoreType.DMA((VIEW,)),
            pltpu.SemaphoreType.DMA((VIEW,)),
            pltpu.SemaphoreType.REGULAR,
            pltpu.SMEM((4, 1, 16), jnp.int32),
            pltpu.SemaphoreType.DMA((3,)),
        ],
        compiler_params=pltpu.CompilerParams(collective_id=0, has_side_effects=True),
    )(velocity, occupied.transpose(0, 2, 1), q_floor, q_span)


def solution(mesh):
    placed = (P(None, "gx", "gy", "view"), P("gx", "gy", "view"), P(), P())
    return jax.shard_map(
        local,
        mesh=mesh,
        in_specs=placed,
        out_specs=P("gx", "gy", None, "view", None),
        check_vma=False,
    )
```
